256 devices in a mesh: seq: 128 (over x, y_lo, z, core), chan: 2 (over y_hi).
Axes of the slice: x: 4, y: 4 (y_hi: 2, y_lo: 2; y = y_hi * 2 + y_lo), z: 8, core: 2. Of those that a mesh axis runs over, the one named last changes fastest.
Arguments:
- tokens: int32 [16384], P('seq'), may hold values from 0 to 3
- stem_weight: bfloat16 [5, 4, 768], replicated, may hold values from -2.5 to 2.5
- conv_weight: bfloat16 [5, 768, 768], P(None, None, 'chan'), may hold values from -0.09375 to 0.09375
- cotangent: bfloat16 [16384, 768], P('seq', 'chan'), may hold values from -6 to 6
Outputs:
- blended: bfloat16 [16384, 768], P('seq', 'chan')
- grad_conv: float32 [5, 768, 768], P(None, 'seq', 'chan')
- grad_stem: float32 [5, 4, 768], P(None, None, 'chan')
The draws below stay inside these ranges and needn't reach their ends.
All inputs are finite; a program needn't handle non-finite values.
Results may differ from the reference program's by a relative error of at most 0.012.
Values may be sent and summed in bfloat16 or wider, within the bound.
A program may use at most 128 MiB of HBM per device.

```python
import math
import jax
import jax.numpy as jnp
from jax import lax

C = 768
KW = 5
LENGTH = 16384


def with_ends(entries, stream_key, smallest, largest):
    spot = [jax.random.randint(jax.random.fold_in(stream_key, axis), (), 0, length) for axis, length in enumerate(entries.shape)]
    widest = entries.shape.index(max(entries.shape))
    beside = spot[:widest] + [(spot[widest] + 1) % entries.shape[widest]] + spot[widest + 1:]
    return entries.at[tuple(spot)].set(smallest).at[tuple(beside)].set(largest)


def steps_of(rng, shape, shards, smallest, high):
    loudness, own = 1.0, jax.random.fold_in(rng, 6)
    for dim, parts in shards:
        steps = jnp.exp(jax.random.uniform(jax.random.fold_in(own, dim), (parts,), jnp.float32, smallest / len(shards), high / len(shards)))
        loudness = loudness * jnp.repeat(steps, shape[dim] // parts).reshape([-1 if axis == dim else 1 for axis in range(len(shape))])
    return loudness


def scatter_about(own_key, shape, scale, bound, shards=(), kind=jnp.bfloat16):
    values = scale * jax.random.normal(own_key, shape, jnp.float32)
    if shards:
        values = values * steps_of(own_key, shape, shards, -0.22, 0.18)
    return jnp.clip(values, -bound, bound).astype(kind)


def setup_inputs(seed: int = 0) -> dict:
    seeds = jax.random.split(jax.random.key(seed), 5)
    return {
        "tokens": with_ends(jax.random.randint(seeds[0], (LENGTH,), 0, 4), jax.random.fold_in(seeds[0], 1), 0, 3).astype(jnp.int32),
        "stem_weight": scatter_about(seeds[1], (KW, 4, C), KW ** -0.5, 2.5),
        "conv_weight": scatter_about(seeds[2], (KW, C, C), (KW * C) ** -0.5, 0.09375, ((2, 2),)),
        "cotangent": scatter_about(seeds[3], (LENGTH, C), 1.0, 6.0, ((0, 128), (1, 2))),
    }


def gelu_parts(values_in):
    coeff = math.sqrt(2.0 / math.pi)
    tanh_val = jnp.tanh(coeff * (values_in + 0.044715 * values_in ** 3))
    result = 0.5 * values_in * (1.0 + tanh_val)
    slopes = 0.5 * (1.0 + tanh_val) + 0.5 * values_in * (1.0 - tanh_val ** 2) * coeff * (1.0 + 3.0 * 0.044715 * values_in ** 2)
    return (result, slopes)

def strand(bases, out_grad, stem_weight, conv_weight):
    count = bases.shape[0]
    one_hot = (bases[:, None] == jnp.arange(4, dtype=jnp.int32)[None, :]).astype(jnp.bfloat16)
    padded_hot = jnp.pad(one_hot, ((2, 2), (0, 0)))
    stem_sum = jnp.zeros((count, stem_weight.shape[2]), jnp.float32)
    for k in range(KW):
        stem_sum = stem_sum + jnp.dot(padded_hot[k:k + count], stem_weight[k], preferred_element_type=jnp.float32)
    stem_act = stem_sum.astype(jnp.bfloat16)
    gelu_val, gelu_slope = gelu_parts(stem_act.astype(jnp.float32))
    act = gelu_val.astype(jnp.bfloat16)
    padded_act = jnp.pad(act, ((2, 2), (0, 0)))
    conv_sum = jnp.zeros((count, conv_weight.shape[2]), jnp.float32)
    for k in range(KW):
        conv_sum = conv_sum + jnp.dot(padded_act[k:k + count], conv_weight[k], preferred_element_type=jnp.float32)
    layer_out = stem_act.astype(jnp.float32) + conv_sum
    padded_grad = jnp.pad(out_grad, ((2, 2), (0, 0)))
    data_grad = jnp.zeros((count, conv_weight.shape[1]), jnp.float32)
    kernel_list = []
    for k in range(KW):
        data_grad = data_grad + jnp.dot(padded_grad[4 - k:4 - k + count], conv_weight[k].T, preferred_element_type=jnp.float32)
        kernel_list.append(jnp.dot(padded_act[k:k + count].T, out_grad, preferred_element_type=jnp.float32))
    stem_grad_in = data_grad * gelu_slope
    stem_list = []
    for k in range(KW):
        stem_list.append(jnp.dot(padded_hot[k:k + count].astype(jnp.float32).T, stem_grad_in, precision=lax.Precision.HIGHEST))
    return (layer_out, jnp.stack(kernel_list), jnp.stack(stem_list))

def reference(tokens, stem_weight, conv_weight, cotangent):
    half_cot = cotangent * 0.5
    out_fwd, kernel_fwd, stem_fwd = strand(tokens, half_cot, stem_weight, conv_weight)
    rc_bases = (3 - tokens[::-1]).astype(jnp.int32)
    out_rev, kernel_rev, stem_rev = strand(rc_bases, half_cot[::-1], stem_weight, conv_weight)
    blended = (0.5 * (out_fwd + out_rev[::-1])).astype(jnp.bfloat16)
    return (blended, kernel_fwd + kernel_rev, stem_fwd + stem_rev)
```

```python
import math

import jax
import jax.numpy as jnp
from jax import lax
from jax.sharding import PartitionSpec as P


def gelu_parts(values_in):
    coeff = math.sqrt(2.0 / math.pi)
    tanh_val = jnp.tanh(coeff * (values_in + 0.044715 * values_in**3))
    result = 0.5 * values_in * (1.0 + tanh_val)
    slopes = 0.5 * (1.0 + tanh_val) + 0.5 * values_in * (1.0 - tanh_val**2) * coeff * (
        1.0 + 3.0 * 0.044715 * values_in**2
    )
    return (result, slopes)


def on_device(tokens, stem_weight, conv_weight, cotangent):
    positions = tokens.shape[0]
    taps, full_width, half_width = conv_weight.shape
    shards = lax.axis_size("seq")
    chan_start = lax.axis_index("chan") * half_width
    grad = cotangent * 0.5
    ids = tokens + 1
    forward = [(i, i + 1) for i in range(shards - 1)]
    backward = [(b, a) for a, b in forward]
    low = lax.ppermute(ids[-4:], "seq", forward)
    high = lax.ppermute(ids[:4], "seq", backward)
    wide = jnp.concatenate([low, ids, high])
    span = positions + 4
    hot = (wide[:, None] == jnp.arange(1, 5, dtype=jnp.int32)[None, :]).astype(jnp.bfloat16)
    hot_f = jnp.concatenate([hot[k : k + span] for k in range(taps)], axis=1)
    hot_r = hot_f[:, ::-1]
    hots = jnp.stack([hot_f, hot_r])
    weight20 = stem_weight.reshape(taps * 4, full_width)
    stem = jnp.einsum("spv,vc->spc", hots, weight20, preferred_element_type=jnp.float32)
    stem = stem.astype(jnp.bfloat16)
    place = lax.axis_index("seq") * positions - 2 + jnp.arange(span, dtype=jnp.int32)
    inside = ((place >= 0) & (place < positions * shards))[None, :, None]
    value, slope = gelu_parts(stem.astype(jnp.float32))
    act = jnp.where(inside, value, 0.0).astype(jnp.bfloat16)
    conv = jnp.zeros((positions, half_width), jnp.float32)
    kernel_list = []
    dact = jnp.zeros((2, span, full_width), jnp.float32)
    for k in range(taps):
        for side, first in ((0, k), (1, 4 - k)):
            rows = act[side, first : first + positions]
            conv = conv + jnp.dot(rows, conv_weight[k], preferred_element_type=jnp.float32)
            both = jnp.dot(rows.T, grad, preferred_element_type=jnp.float32)
            kernel_list.append(both)
        part = jnp.einsum("pd,cd->pc", grad, conv_weight[k], preferred_element_type=jnp.float32)
        dact = dact + jnp.stack(
            [jnp.pad(part, ((k, 4 - k), (0, 0))), jnp.pad(part, ((4 - k, k), (0, 0)))]
        )
    own_stem = lax.dynamic_slice_in_dim(stem[:, 2 : positions + 2], chan_start, half_width, 2)
    own_stem = own_stem.astype(jnp.float32)
    blended = (0.5 * (own_stem[0] + own_stem[1] + conv)).astype(jnp.bfloat16)
    dstem = jnp.where(inside, dact * slope, 0.0)
    stem_grad = jnp.einsum(
        "spv,spc->vc", hots.astype(jnp.float32), dstem, precision=lax.Precision.HIGHEST
    )
    stem_grad = lax.psum(stem_grad, ("seq", "chan"))
    stem_grad = lax.dynamic_slice_in_dim(stem_grad, chan_start, half_width, 1)
    grad_conv = lax.psum_scatter(jnp.stack(kernel_list[0::2]) + jnp.stack(kernel_list[1::2]), "seq", scatter_dimension=1, tiled=True)
    return (blended, grad_conv, stem_grad.reshape(taps, 4, half_width))


def solution(mesh):
    return jax.shard_map(
        on_device,
        mesh=mesh,
        in_specs=(P("seq"), P(), P(None, None, "chan"), P("seq", "chan")),
        out_specs=(P("seq", "chan"), P(None, "seq", "chan"), P(None, None, "chan")),
        check_vma=False,
    )
```

```python
import math

import jax
import jax.numpy as jnp
from jax import lax
from jax.experimental import pallas as pl
from jax.experimental.pallas import tpu as pltpu
from jax.sharding import PartitionSpec as P

F32, BF16, I32 = jnp.float32, jnp.bfloat16, jnp.int32
C0 = math.sqrt(2.0 / math.pi)
C1 = C0 * 0.044715
OUTSIDE = 4
FAR_FIRST = (4, 3, 5, 2, 6, 1, 7, 0)
ROWS, FULL, HALF, TAPS = 128, 768, 384, 5
NX, NY, NZ = 4, 2, 8


def dot(a, b, dims):
    return lax.dot_general(a, b, (dims, ((), ())), preferred_element_type=F32)


def rounded(v):
    return v.astype(BF16).astype(F32)


def kernel(
    tok_ref, sw_ref, w_hbm, cot_ref,
    bl_ref, gc_ref, gs_ref,
    w_ref, toks, wins, gall, w40, w40b, sel_ref, ohf, stm, grow, skb, dsh, dsl, conv,
    stt, st, gsacc, rsend, rown, ry, zsend, zrecv,
    gsend, gchan, gsum, grz, gone, grx, gry, gfin, gtile,
    wsem, ssem, rsem,
):
    seq, chan = lax.axis_index("seq"), lax.axis_index("chan")
    core = lax.rem(seq, 2)
    z = lax.rem(lax.div(seq, 2), NZ)
    y = lax.rem(lax.div(seq, 2 * NZ), NY)
    x = lax.div(seq, 2 * NZ * NY)

    def at(px, py, pz, pc):
        return (((px * NY + py) * NZ + pz) * 2 + pc, chan)

    def x_by(d):
        return at(lax.rem(x + d, NX), y, z, core)

    def z_by(d):
        return at(x, y, lax.rem(z + d, NZ), core)

    sibling = at(x, y, z, 1 - core)
    beside_y = at(x, 1 - y, z, core)
    across = at(x, 1 - y, z, 1 - core)
    outer = (lax.rem(seq + 128 + 2 * core - 1, 128), chan)
    other_chan = (seq, 1 - chan)
    partners = [sibling, beside_y, across, outer, other_chan]
    partners += [x_by(d) for d in range(1, NX)] + [z_by(d) for d in range(1, NZ)]

    used = []

    def send(src, dst, device):
        n = len(used)
        copy = pltpu.make_async_remote_copy(
            src_ref=src, dst_ref=dst, send_sem=ssem.at[n], recv_sem=rsem.at[n],
            device_id=device, device_id_type=pl.DeviceIdType.MESH,
        )
        copy.start()
        used.append(copy)
        return copy

    loads = [pltpu.make_async_copy(w_hbm.at[k], w_ref.at[k], wsem.at[k]) for k in range(TAPS)]
    for load in loads:
        load.start()

    barrier = pltpu.get_barrier_semaphore()
    for device in partners:
        pl.semaphore_signal(
            barrier, inc=1, device_id=device, device_id_type=pl.DeviceIdType.MESH
        )

    toks[0] = jnp.broadcast_to(tok_ref[...], (8, ROWS))
    gall[0] = cot_ref[...]
    w40[...] = jnp.zeros_like(w40)
    for j in range(TAPS):
        w40[8 * j : 8 * j + 4, :] = sw_ref[j].astype(F32)
    w40[20:21, :] = jnp.full((1, FULL), -128.0, F32)
    w40b[...] = w40[...].astype(BF16)
    ohf[...] = jnp.zeros_like(ohf)
    gsacc[...] = jnp.zeros_like(gsacc)

    row = lax.broadcasted_iota(I32, (512, 1), 0)
    rest = row & 31
    tap = (rest * 43) >> 8
    place = (row >> 5) & 7
    step = jnp.zeros_like(row)
    for n, d in enumerate(FAR_FIRST):
        step = jnp.where(place == n, d, step)
    zrow = (z + step) & 7
    yrow = jnp.where(row < 256, 1 - y, y)
    col = 192 * x + 96 * yrow + 12 * zrow + 6 * core + rest - 6 * tap
    col = jnp.where(tap < TAPS, col, -1)
    lane = lax.broadcasted_iota(I32, (512, FULL), 1)
    chosen = jnp.where(lane == col, 1.0, 0.0).astype(BF16)
    table = dot(chosen, w40b[...], ((1,), (1,)))
    placed = jnp.zeros((512, 128), F32)
    for k in range(TAPS):
        moved = table if k == 0 else pltpu.roll(table, 8 * k, 1)
        placed = jnp.where(tap == k, moved, placed)
    sel_ref[...] = placed.astype(BF16)

    pl.semaphore_wait(barrier, len(partners))

    tok_sib = send(toks.at[0], toks.at[1], sibling)
    tok_out = send(toks.at[0], toks.at[2], outer)
    g_x = {d: send(gall.at[0], gall.at[d], x_by(d)) for d in (2, 1, 3)}
    g_sib = {0: send(gall.at[0], gall.at[4], sibling)}

    tok_sib.wait_recv()
    tok_out.wait_recv()
    near, far = toks[1], toks[2]
    left = jnp.where(core == 1, near, far)
    right = jnp.where(core == 1, far, near)
    left = jnp.where(seq == 0, OUTSIDE, left)
    right = jnp.where(seq == 127, OUTSIDE, right)
    row3 = jnp.concatenate([left, toks[0], right], axis=1)
    wins[0] = pltpu.roll(row3, 3 * ROWS - 124, 1)[:, :256]
    win_x = {d: send(wins.at[0], wins.at[d], x_by(d)) for d in (2, 1, 3)}
    win_sib = {0: send(wins.at[0], wins.at[4], sibling)}

    letter = lax.broadcasted_iota(I32, (8, ROWS), 0)

    def one_hots(b):
        win = wins[b]
        for i in range(9):
            ids = win[:, :ROWS] if i == 0 else pltpu.roll(win, 256 - i, 1)[:, :ROWS]
            ohf[8 * i : 8 * i + 8, :ROWS] = jnp.where(ids == letter, 1.0, 0.0)
            turned = jnp.where(ids == OUTSIDE, OUTSIDE, 3 - ids)
            ohf[64 - 8 * i : 72 - 8 * i, ROWS:] = jnp.where(turned == letter, 1.0, 0.0)

    one_hots(0)

    def own_tap(k):
        loads[k].wait()
        hot = ohf[8 * k : 8 * k + 40, :].astype(BF16)
        stm[...] = dot(hot, w40b[0:40, :], ((0,), (0,)))
        grow[...] = dot(gall[0], w_ref[k], ((1,), (1,)))
        if k == 2:
            mine = pl.ds(pl.multiple_of(chan * HALF, 128), HALF)
            conv[...] += rounded(stm[0:ROWS, mine]) + rounded(stm[ROWS:, mine])

        def strip(n, _):
            top = pl.ds(pl.multiple_of(n * 16, 16), 16)
            low = pl.ds(pl.multiple_of(n * 16 + ROWS, 16), 16)
            for c in range(0, FULL, 256):
                cols = slice(c, c + 256)
                grad = grow[top, cols]
                total = None
                for part in (top, low):
                    v = rounded(stm[part, cols])
                    v2 = v * v
                    h = 0.5 + 0.5 * jnp.tanh(v * (C0 + C1 * v2))
                    act = v * h
                    total = act if total is None else total + act
                    slope = h + (2.0 * h) * (1.0 - h) * (v * (C0 + 3.0 * C1 * v2))
                    ds = grad * slope
                    big = ds.astype(BF16)
                    dsh[part, cols] = big
                    dsl[part, cols] = (ds - big.astype(F32)).astype(BF16)
                skb[top, cols] = total.astype(BF16)
            return 0

        lax.fori_loop(0, ROWS // 16, strip, 0)
        conv[...] += dot(skb[...], w_ref[k], ((1,), (0,)))
        gsacc[...] += dot(hot, dsh[...], ((1,), (0,))) + dot(hot, dsl[...], ((1,), (0,)))

    conv[...] = jnp.zeros_like(conv)
    own_tap(0)
    for d in (1, 3, 2):
        win_x[d].wait_recv()
        win_sib[d] = send(wins.at[d], wins.at[4 + d], sibling)
    own_tap(1)
    own_tap(2)
    for d in (1, 3):
        g_x[d].wait_recv()
        g_sib[d] = send(gall.at[d], gall.at[4 + d], sibling)
    own_tap(3)
    own_tap(4)
    g_x[2].wait_recv()
    g_sib[2] = send(gall.at[2], gall.at[6], sibling)
    bl_ref[...] = (0.5 * conv[...]).astype(BF16)

    for j in range(TAPS):
        for t in range(3):
            here = pl.ds(pl.multiple_of(chan * HALF + 128 * t, 128), 128)
            there = pl.ds(pl.multiple_of((1 - chan) * HALF + 128 * t, 128), 128)
            gsum[3 * j + t] = gsacc[8 * j : 8 * j + 8, here]
            gsend[3 * j + t] = gsacc[8 * j : 8 * j + 8, there]
    gsum[15] = jnp.zeros((8, 128), F32)
    gsend[15] = jnp.zeros((8, 128), F32)
    s_chan = send(gsend, gchan, other_chan)

    def block(b):
        if b:
            one_hots(b)
        stt[...] = dot(sel_ref[...], ohf[...].astype(BF16), ((1,), (0,)))

        def strip(n, _):
            rows = pl.ds(pl.multiple_of(n * 16, 16), 16)
            v = rounded(stt[rows, :])
            act = v * (0.5 + 0.5 * jnp.tanh(v * (C0 + C1 * (v * v))))
            st[rows, b * ROWS : (b + 1) * ROWS] = (act[:, :ROWS] + act[:, ROWS:]).astype(BF16)
            return 0

        lax.fori_loop(0, 512 // 16, strip, 0, unroll=4)

    block(0)
    for d in (1, 2, 3):
        block(d)
    for d in range(4):
        win_sib[d].wait_recv()
        block(4 + d)

    s_chan.wait_recv()
    gsum[...] += gchan[...]
    s_z = [
        send(gsum.at[pl.ds(2 * lax.rem(z + d, NZ), 2)], grz.at[d], z_by(d)) for d in range(1, NZ)
    ]

    for d in range(4):
        g_sib[d].wait_recv()
    every = gall[...].reshape(8 * ROWS, HALF)
    s_y = []
    for n in range(4):
        rows = slice(64 * n, 64 * n + 64)
        rsend[rows, :] = dot(st[rows, :], every, ((1,), (0,))).astype(BF16)
        s_y.append(send(rsend.at[pl.ds(64 * n, 64)], ry.at[pl.ds(64 * n, 64)], beside_y))
    rown[...] = dot(st[256:, :], every, ((1,), (0,)))

    for copy in s_z:
        copy.wait_recv()
    part = gsum[pl.ds(2 * z, 2)]
    for d in range(1, NZ):
        part = part + grz[d]
    gone[...] = part
    grx[x] = part
    s_gx = [send(gone, grx.at[x], x_by(d)) for d in range(1, NX)]

    s_rz = []
    for n in range(4):
        s_y[n].wait_recv()
        rows = slice(64 * n, 64 * n + 64)
        both = rown[rows, :] + ry[rows, :].astype(F32)
        if n == 3:
            rown[rows, :] = both
        zsend[rows, :] = both.astype(BF16)
        for m in (2 * n, 2 * n + 1):
            d = FAR_FIRST[m]
            if d:
                s_rz.append(send(zsend.at[pl.ds(32 * m, 32)], zrecv.at[d], z_by(d)))

    for copy in s_gx:
        copy.wait_recv()
    part = (grx[0] + grx[1]) + (grx[2] + grx[3])
    gtile[...] = part
    me = 2 * y + core
    gry[me] = part
    s_gy = [send(gtile, gry.at[me], device) for device in (sibling, beside_y, across)]
    for copy in s_gy:
        copy.wait_recv()
    part = 0.5 * ((gry[0] + gry[1]) + (gry[2] + gry[3]))
    gfin[pl.ds(2 * z, 2)] = part
    s_gf = [
        send(gfin.at[pl.ds(2 * z, 2)], gfin.at[pl.ds(2 * z, 2)], z_by(d)) for d in range(1, NZ)
    ]

    for copy in s_rz:
        copy.wait_recv()
    total = rown[224:256, :]
    for d in range(1, NZ):
        total = total + zrecv[d].astype(F32)
    total = 0.5 * total
    for k in range(TAPS):
        gc_ref[k] = total[6 * k : 6 * k + 6, :]
    for copy in s_gf:
        copy.wait_recv()
    for j in range(TAPS):
        for t in range(3):
            gs_ref[j, :, 128 * t : 128 * t + 128] = gfin[3 * j + t, 0:4, :]
    for copy in used:
        copy.wait_send()


def on_device(tokens, stem_weight, conv_weight, cotangent):
    vmem = pl.BlockSpec(memory_space=pltpu.VMEM)
    V = pltpu.VMEM
    return pl.pallas_call(
        kernel,
        out_shape=(
            jax.ShapeDtypeStruct((ROWS, HALF), BF16),
            jax.ShapeDtypeStruct((TAPS, 6, HALF), F32),
            jax.ShapeDtypeStruct((TAPS, 4, HALF), F32),
        ),
        in_specs=[vmem, vmem, pl.BlockSpec(memory_space=pl.ANY), vmem],
        out_specs=(vmem, vmem, vmem),
        scratch_shapes=[
            V((TAPS, FULL, HALF), BF16), V((3, 8, ROWS), I32), V((8, 8, 256), I32),
            V((8, ROWS, HALF), BF16), V((128, FULL), F32), V((128, FULL), BF16),
            V((512, 128), BF16), V((128, 256), F32), V((256, FULL), F32), V((ROWS, FULL), F32),
            V((ROWS, FULL), BF16), V((256, FULL), BF16), V((256, FULL), BF16), V((ROWS, HALF), F32),
            V((512, 256), F32), V((512, 1024), BF16), V((40, FULL), F32), V((256, HALF), BF16),
            V((256, HALF), F32), V((256, HALF), BF16), V((256, HALF), BF16), V((8, 32, HALF), BF16),
            V((16, 8, 128), F32), V((16, 8, 128), F32), V((16, 8, 128), F32), V((8, 2, 8, 128), F32),
            V((2, 8, 128), F32), V((4, 2, 8, 128), F32), V((4, 2, 8, 128), F32),
            V((16, 8, 128), F32), V((2, 8, 128), F32),
            pltpu.SemaphoreType.DMA((TAPS,)), pltpu.SemaphoreType.DMA((64,)),
            pltpu.SemaphoreType.DMA((64,)),
        ],
        compiler_params=pltpu.CompilerParams(
            collective_id=0, has_side_effects=True, vmem_limit_bytes=48 * 2**20
        ),
    )(tokens.reshape(1, ROWS), stem_weight, conv_weight, cotangent)


def solution(mesh):
    return jax.shard_map(
        on_device,
        mesh=mesh,
        in_specs=(P("seq"), P(), P(None, None, "chan"), P("seq", "chan")),
        out_specs=(P("seq", "chan"), P(None, "seq", "chan"), P(None, None, "chan")),
        check_vma=False,
    )
```

```python
import math

import jax
import jax.numpy as jnp
from jax import lax
from jax.experimental import pallas as pl
from jax.experimental.pallas import tpu as pltpu
from jax.sharding import PartitionSpec as P

F32, BF16, I32 = jnp.float32, jnp.bfloat16, jnp.int32
C0 = math.sqrt(2.0 / math.pi)
C1 = C0 * 0.044715
OUTSIDE = 4
FAR_FIRST = (4, 3, 5, 2, 6, 1, 7, 0)
ROWS, FULL, HALF, TAPS = 128, 768, 384, 5
NX, NY, NZ = 4, 2, 8


def dot(a, b, dims):
    return lax.dot_general(a, b, (dims, ((), ())), preferred_element_type=F32)


def rounded(v):
    return v.astype(BF16).astype(F32)


def gelu_half(v, v2):
    return 0.5 + 0.5 * jnp.tanh(v * (C0 + C1 * v2))


def kernel(
    tok_hbm, sw_hbm, w_hbm, cot_hbm,
    bl_ref, gc_ref, gs_ref,
    w_ref, tok_ref, sw_ref, toks, wins, gall, w40, w40b, sel_ref, ohf, ohb, hots, stm, grow, skb, dsb,
    stt, st, rsend, rown, ry, zsend, zrecv,
    gsend, grz, gone, grx, gfin,
    wsem, ssem, rsem,
):
    seq, chan = lax.axis_index("seq"), lax.axis_index("chan")
    core = lax.rem(seq, 2)
    z = lax.rem(lax.div(seq, 2), NZ)
    y = lax.rem(lax.div(seq, 2 * NZ), NY)
    x = lax.div(seq, 2 * NZ * NY)

    def at(px, py, pz, pc, ch):
        return (((px * NY + py) * NZ + pz) * 2 + pc, ch)

    def x_by(d):
        return at(lax.rem(x + d, NX), y, z, core, chan)

    def z_by(d, other=0):
        return at(x, y, lax.rem(z + d, NZ), core, 1 - chan if other else chan)

    def across(dx, dy, dc):
        return at(
            lax.rem(x + dx, NX), 1 - y if dy else y, z, 1 - core if dc else core, chan
        )

    sibling = across(0, 0, 1)
    beside_y = across(0, 1, 0)
    outer = (lax.rem(seq + 128 + 2 * core - 1, 128), chan)
    shifts = [(dx, dy, dc) for dx in (2, 1, 3, 0) for dy in (1, 0) for dc in (1, 0)][:-1]
    z_steps = [(d, other) for other in (1, 0) for d in FAR_FIRST][:-1]
    partners = [outer] + [across(*s) for s in shifts] + [z_by(*s) for s in z_steps]

    barrier = pltpu.get_barrier_semaphore()
    for device in partners:
        pl.semaphore_signal(
            barrier, inc=1, device_id=device, device_id_type=pl.DeviceIdType.MESH
        )

    used = []

    def send(src, dst, device):
        n = len(used)
        copy = pltpu.make_async_remote_copy(
            src_ref=src, dst_ref=dst, send_sem=ssem.at[n], recv_sem=rsem.at[n],
            device_id=device, device_id_type=pl.DeviceIdType.MESH,
        )
        copy.start()
        used.append(copy)
        return copy

    def load(n, src, dst):
        copy = pltpu.make_async_copy(src, dst, wsem.at[n])
        copy.start()
        return copy

    load_tok = load(5, tok_hbm, tok_ref)
    load_sw = load(6, sw_hbm, sw_ref)
    load_cot = load(7, cot_hbm, gall.at[0])
    loads = [load(k, w_hbm.at[k], w_ref.at[k]) for k in range(TAPS)]

    w40[...] = jnp.zeros_like(w40)
    ohf[...] = jnp.zeros_like(ohf)
    load_tok.wait()
    toks[0] = jnp.broadcast_to(tok_ref[...], (8, ROWS))
    load_cot.wait()
    pl.semaphore_wait(barrier, len(partners))

    tok_sib = send(toks.at[0], toks.at[1], sibling)
    tok_out = send(toks.at[0], toks.at[2], outer)
    g_x = {d: send(gall.at[0], gall.at[d], x_by(d)) for d in (1, 3)}
    g_sib = {0: send(gall.at[0], gall.at[4], sibling)}

    load_sw.wait()
    for j in range(TAPS):
        w40[8 * j : 8 * j + 4, :] = sw_ref[j].astype(F32)
    w40[20:21, :] = jnp.full((1, FULL), -128.0, F32)
    w40b[...] = w40[...].astype(BF16)

    row = lax.broadcasted_iota(I32, (512, 1), 0)
    rest = row & 31
    tap = (rest * 43) >> 8
    place = (row >> 5) & 7
    step = jnp.zeros_like(row)
    for n, d in enumerate(FAR_FIRST):
        step = jnp.where(place == n, d, step)
    zrow = (z + step) & 7
    yrow = jnp.where(row < 256, 1 - y, y)
    col = 192 * x + 96 * yrow + 12 * zrow + 6 * core + rest - 6 * tap
    col = jnp.where(tap < TAPS, col, -1)
    lane = lax.broadcasted_iota(I32, (512, FULL), 1)
    chosen = jnp.where(lane == col, 1.0, 0.0).astype(BF16)
    table = dot(chosen, w40b[...], ((1,), (1,)))
    placed = jnp.zeros((512, 128), F32)
    for k in range(TAPS):
        moved = table if k == 0 else pltpu.roll(table, 8 * k, 1)
        placed = jnp.where(tap == k, moved, placed)
    sel_ref[...] = placed.astype(BF16)

    for k in range(TAPS):
        loads[k].wait()
        grow[:, FULL * k : FULL * (k + 1)] = dot(gall[0], w_ref[k], ((1,), (1,)))

    tok_sib.wait_recv()
    tok_out.wait_recv()
    near, far = toks[1], toks[2]
    left = jnp.where(core == 1, near, far)
    right = jnp.where(core == 1, far, near)
    left = jnp.where(seq == 0, OUTSIDE, left)
    right = jnp.where(seq == 127, OUTSIDE, right)
    row3 = jnp.concatenate([left, toks[0], right], axis=1)
    wins[0] = pltpu.roll(row3, 3 * ROWS - 124, 1)[:, :256]
    win_x = {d: send(wins.at[0], wins.at[d], x_by(d)) for d in (2, 1, 3)}
    win_sib = {0: send(wins.at[0], wins.at[4], sibling)}

    letter = lax.broadcasted_iota(I32, (8, ROWS), 0)

    def one_hots(b):
        win = wins[b]
        for i in range(9):
            ids = win[:, :ROWS] if i == 0 else pltpu.roll(win, 256 - i, 1)[:, :ROWS]
            ohf[8 * i : 8 * i + 8, :ROWS] = jnp.where(ids == letter, 1.0, 0.0)
            turned = jnp.where(ids == OUTSIDE, OUTSIDE, 3 - ids)
            ohf[64 - 8 * i : 72 - 8 * i, ROWS:] = jnp.where(turned == letter, 1.0, 0.0)
        ohb[:, 256 * b : 256 * b + 256] = ohf[...].astype(BF16)

    one_hots(0)
    for k in range(TAPS):
        hots[:, 256 * k : 256 * k + 256] = ohf[8 * k : 8 * k + 40, :].astype(BF16)

    def own_tap(k):
        hot = hots[:, 256 * k : 256 * k + 256]
        stm[...] = dot(hot, w40b[0:40, :], ((0,), (0,)))
        if k == 2:
            mine = pl.ds(pl.multiple_of(chan * HALF, 128), HALF)
            rown[0:ROWS, :] = rounded(stm[0:ROWS, mine]) + rounded(stm[ROWS:, mine])

        def strip(n, _):
            top = pl.ds(pl.multiple_of(n * 32, 32), 32)
            for c in range(0, FULL, 256):
                cols = slice(c, c + 256)
                wide = slice(FULL * k + c, FULL * k + c + 256)
                grad = grow[top, wide]
                total = None
                for side in range(2):
                    v = rounded(stm[pl.ds(pl.multiple_of(n * 32 + ROWS * side, 32), 32), cols])
                    v2 = v * v
                    h = gelu_half(v, v2)
                    act = v * h
                    total = act if total is None else total + act
                    slope = h + (act - act * h) * (2.0 * C0 + 6.0 * C1 * v2)
                    into = pl.ds(pl.multiple_of(n * 32 + 256 * k + ROWS * side, 32), 32)
                    dsb[into, cols] = (grad * slope).astype(BF16)
                skb[top, wide] = total.astype(BF16)
            return 0

        lax.fori_loop(0, ROWS // 32, strip, 0)

    own_tap(0)
    own_tap(1)
    for d in (1, 3, 2):
        win_x[d].wait_recv()
        win_sib[d] = send(wins.at[d], wins.at[4 + d], sibling)
    own_tap(2)
    halves = []
    for d, half in ((1, 0), (3, 1)):
        g_x[d].wait_recv()
        rows = pl.ds(64 * half, 64)
        halves.append(send(gall.at[d, rows], gall.at[2, rows], x_by(d)))
        g_sib[d] = send(gall.at[d], gall.at[4 + d], sibling)
    own_tap(3)
    own_tap(4)
    for copy in halves:
        copy.wait_recv()
    g_sib[2] = send(gall.at[2], gall.at[6], sibling)

    gsacc = dot(hots[...], dsb[...], ((1,), (0,)))
    for h in range(2):
        for j in range(TAPS):
            for t in range(3):
                c = HALF * h + 128 * t
                gsend[h, 3 * j + t] = gsacc[8 * j : 8 * j + 8, c : c + 128]
        gsend[h, 15] = jnp.zeros((8, 128), F32)
    s_z = []
    for d, other in z_steps:
        part = gsend.at[1 - chan if other else chan, pl.ds(2 * lax.rem(z + d, NZ), 2)]
        s_z.append(send(part, grz.at[8 * other + d], z_by(d, other)))

    def blocks(first):
        here = slice(256 * first, 256 * first + 1024)
        stt[...] = dot(sel_ref[...], ohb[:, here], ((1,), (0,)))

        def strip(n, _):
            rows = pl.ds(pl.multiple_of(n * 64, 64), 64)
            for b in range(4):
                v = rounded(stt[rows, 256 * b : 256 * b + 256])
                act = v * gelu_half(v, v * v)
                into = slice((first + b) * ROWS, (first + b + 1) * ROWS)
                st[rows, into] = (act[:, :ROWS] + act[:, ROWS:]).astype(BF16)
            return 0

        lax.fori_loop(0, 512 // 64, strip, 0)

    for b in range(1, 4):
        one_hots(b)
    blocks(0)
    for d in range(4):
        win_sib[d].wait_recv()
        one_hots(4 + d)
    blocks(4)

    for d in range(4):
        g_sib[d].wait_recv()
    every = gall[...].reshape(8 * ROWS, HALF)
    s_y = []
    for n in range(4):
        rows = slice(64 * n, 64 * n + 64)
        rsend[rows, :] = dot(st[rows, :], every, ((1,), (0,))).astype(BF16)
        s_y.append(send(rsend.at[pl.ds(64 * n, 64)], ry.at[pl.ds(64 * n, 64)], beside_y))
    conv = rown[0:ROWS, :]
    conv += dot(skb[...], w_ref[...].reshape(TAPS * FULL, HALF), ((1,), (0,)))
    bl_ref[...] = (0.5 * conv).astype(BF16)
    rown[...] = dot(st[256:, :], every, ((1,), (0,)))

    for copy in s_z:
        copy.wait_recv()
    part = gsend[chan, pl.ds(2 * z, 2)]
    for d, other in z_steps:
        part = part + grz[8 * other + d]
    gone[...] = part
    me = 4 * x + 2 * y + core
    grx[me] = part
    s_gx = [send(gone, grx.at[me], across(*s)) for s in shifts]

    s_rz = []
    for n in range(4):
        s_y[n].wait_recv()
        rows = slice(64 * n, 64 * n + 64)
        both = rown[rows, :] + ry[rows, :].astype(F32)
        if n == 3:
            rown[rows, :] = both
        zsend[rows, :] = both.astype(BF16)
        for m in (2 * n, 2 * n + 1):
            d = FAR_FIRST[m]
            if d:
                s_rz.append(send(zsend.at[pl.ds(32 * m, 32)], zrecv.at[d], z_by(d)))

    for copy in s_gx:
        copy.wait_recv()
    parts = [grx[n] for n in range(16)]
    while len(parts) > 1:
        parts = [p + q for p, q in zip(parts[0::2], parts[1::2])]
    gfin[pl.ds(2 * z, 2)] = 0.5 * parts[0]
    s_gf = [
        send(gfin.at[pl.ds(2 * z, 2)], gfin.at[pl.ds(2 * z, 2)], z_by(d)) for d in range(1, NZ)
    ]

    for copy in s_rz:
        copy.wait_recv()
    total = rown[224:256, :]
    for d in range(1, NZ):
        total = total + zrecv[d].astype(F32)
    total = 0.5 * total
    for k in range(TAPS):
        gc_ref[k] = total[6 * k : 6 * k + 6, :]
    for copy in s_gf:
        copy.wait_recv()
    for j in range(TAPS):
        for t in range(3):
            gs_ref[j, :, 128 * t : 128 * t + 128] = gfin[3 * j + t, 0:4, :]
    for copy in used:
        copy.wait_send()


def on_device(tokens, stem_weight, conv_weight, cotangent):
    vmem = pl.BlockSpec(memory_space=pltpu.VMEM)
    hbm = pl.BlockSpec(memory_space=pltpu.HBM)
    V = pltpu.VMEM
    return pl.pallas_call(
        kernel,
        out_shape=(
            jax.ShapeDtypeStruct((ROWS, HALF), BF16),
            jax.ShapeDtypeStruct((TAPS, 6, HALF), F32),
            jax.ShapeDtypeStruct((TAPS, 4, HALF), F32),
        ),
        in_specs=[hbm, hbm, hbm, hbm],
        out_specs=(vmem, vmem, vmem),
        scratch_shapes=[
            V((TAPS, FULL, HALF), BF16), V((1, ROWS), I32), V((TAPS, 4, FULL), BF16),
            V((3, 8, ROWS), I32), V((8, 8, 256), I32),
            V((8, ROWS, HALF), BF16), V((128, FULL), F32), V((128, FULL), BF16),
            V((512, 128), BF16), V((128, 256), F32), V((128, 2048), BF16), V((40, 1280), BF16),
            V((256, FULL), F32), V((ROWS, TAPS * FULL), F32),
            V((ROWS, TAPS * FULL), BF16), V((TAPS * 256, FULL), BF16),
            V((512, 1024), F32), V((512, 1024), BF16), V((256, HALF), BF16),
            V((256, HALF), F32), V((256, HALF), BF16), V((256, HALF), BF16), V((8, 32, HALF), BF16),
            V((2, 16, 8, 128), F32), V((16, 2, 8, 128), F32),
            V((2, 8, 128), F32), V((16, 2, 8, 128), F32), V((16, 8, 128), F32),
            pltpu.SemaphoreType.DMA((8,)), pltpu.SemaphoreType.DMA((80,)),
            pltpu.SemaphoreType.DMA((80,)),
        ],
        compiler_params=pltpu.CompilerParams(
            collective_id=0, has_side_effects=True, vmem_limit_bytes=48 * 2**20
        ),
    )(tokens.reshape(1, ROWS), stem_weight, conv_weight, cotangent)


def solution(mesh):
    return jax.shard_map(
        on_device,
        mesh=mesh,
        in_specs=(P("seq"), P(), P(None, None, "chan"), P("seq", "chan")),
        out_specs=(P("seq", "chan"), P(None, "seq", "chan"), P(None, None, "chan")),
        check_vma=False,
    )
```

```python
import math

import jax
import jax.numpy as jnp
from jax import lax
from jax.experimental import pallas as pl
from jax.experimental.pallas import tpu as pltpu
from jax.sharding import PartitionSpec as P

F32, BF16, I32 = jnp.float32, jnp.bfloat16, jnp.int32
C0 = math.sqrt(2.0 / math.pi)
C1 = C0 * 0.044715
OUTSIDE = 4
FAR_FIRST = (4, 3, 5, 2, 6, 1, 7, 0)
ROWS, FULL, HALF, TAPS = 128, 768, 384, 5
NX, NY, NZ = 4, 2, 8


def dot(a, b, dims):
    return lax.dot_general(a, b, (dims, ((), ())), preferred_element_type=F32)


def rounded(v):
    return v.astype(BF16).astype(F32)


def gelu_half(v, v2):
    return 0.5 + 0.5 * jnp.tanh(v * (C0 + C1 * v2))


def kernel(
    tok_hbm, sw_hbm, w_hbm, cot_hbm,
    bl_ref, gc_ref, gs_ref,
    w_ref, tok_ref, sw_ref, toks, wins, gall, w40, w40b, sel_ref, ohf, ohb, hots, stm, grow, skb, dsb,
    stt, st, rsend, rown, ry, zsend, zrecv,
    gsend, grz, gone, grx, gfin,
    wsem, ssem, rsem,
):
    seq, chan = lax.axis_index("seq"), lax.axis_index("chan")
    core = lax.rem(seq, 2)
    z = lax.rem(lax.div(seq, 2), NZ)
    y = lax.rem(lax.div(seq, 2 * NZ), NY)
    x = lax.div(seq, 2 * NZ * NY)

    def at(px, py, pz, pc, ch):
        return (((px * NY + py) * NZ + pz) * 2 + pc, ch)

    def x_by(d):
        return at(lax.rem(x + d, NX), y, z, core, chan)

    def z_by(d, other=0):
        return at(x, y, lax.rem(z + d, NZ), core, 1 - chan if other else chan)

    def across(dx, dy, dc):
        return at(
            lax.rem(x + dx, NX), 1 - y if dy else y, z, 1 - core if dc else core, chan
        )

    sibling = across(0, 0, 1)
    beside_y = across(0, 1, 0)
    outer = (lax.rem(seq + 128 + 2 * core - 1, 128), chan)
    shifts = [(dx, dy, dc) for dx in (2, 1, 3, 0) for dy in (1, 0) for dc in (1, 0)][:-1]
    z_steps = [(d, other) for other in (1, 0) for d in FAR_FIRST][:-1]
    partners = [outer] + [across(*s) for s in shifts] + [z_by(*s) for s in z_steps]

    barrier = pltpu.get_barrier_semaphore()
    for device in partners:
        pl.semaphore_signal(
            barrier, inc=1, device_id=device, device_id_type=pl.DeviceIdType.MESH
        )

    used = []

    def send(src, dst, device):
        n = len(used)
        copy = pltpu.make_async_remote_copy(
            src_ref=src, dst_ref=dst, send_sem=ssem.at[n], recv_sem=rsem.at[n],
            device_id=device, device_id_type=pl.DeviceIdType.MESH,
        )
        copy.start()
        used.append(copy)
        return copy

    def load(n, src, dst):
        copy = pltpu.make_async_copy(src, dst, wsem.at[n])
        copy.start()
        return copy

    load_tok = load(5, tok_hbm, tok_ref)
    load_sw = load(6, sw_hbm, sw_ref)
    load_cot = load(7, cot_hbm, gall.at[0])
    loads = [load(k, w_hbm.at[k], w_ref.at[k]) for k in range(TAPS)]

    w40[...] = jnp.zeros_like(w40)
    ohf[...] = jnp.zeros_like(ohf)
    load_tok.wait()
    toks[0] = jnp.broadcast_to(tok_ref[...], (8, ROWS))
    load_cot.wait()
    pl.semaphore_wait(barrier, len(partners))

    tok_sib = send(toks.at[0], toks.at[1], sibling)
    tok_out = send(toks.at[0], toks.at[2], outer)
    g_x = {d: send(gall.at[0], gall.at[d], x_by(d)) for d in (1, 3)}
    g_sib = {0: send(gall.at[0], gall.at[4], sibling)}

    load_sw.wait()
    for j in range(TAPS):
        w40[8 * j : 8 * j + 4, :] = sw_ref[j].astype(F32)
    w40[20:21, :] = jnp.full((1, FULL), -128.0, F32)
    w40b[...] = w40[...].astype(BF16)

    row = lax.broadcasted_iota(I32, (512, 1), 0)
    rest = row & 31
    tap = (rest * 43) >> 8
    place = (row >> 5) & 7
    step = jnp.zeros_like(row)
    for n, d in enumerate(FAR_FIRST):
        step = jnp.where(place == n, d, step)
    zrow = (z + step) & 7
    yrow = jnp.where(row < 256, 1 - y, y)
    col = 192 * x + 96 * yrow + 12 * zrow + 6 * core + rest - 6 * tap
    col = jnp.where(tap < TAPS, col, -1)
    lane = lax.broadcasted_iota(I32, (512, FULL), 1)
    chosen = jnp.where(lane == col, 1.0, 0.0).astype(BF16)
    table = dot(chosen, w40b[...], ((1,), (1,)))
    placed = jnp.zeros((512, 128), F32)
    for k in range(TAPS):
        moved = table if k == 0 else pltpu.roll(table, 8 * k, 1)
        placed = jnp.where(tap == k, moved, placed)
    sel_ref[...] = placed.astype(BF16)

    for k in range(TAPS):
        loads[k].wait()
        grow[:, FULL * k : FULL * (k + 1)] = dot(gall[0], w_ref[k], ((1,), (1,)))

    tok_sib.wait_recv()
    tok_out.wait_recv()
    near, far = toks[1], toks[2]
    left = jnp.where(core == 1, near, far)
    right = jnp.where(core == 1, far, near)
    left = jnp.where(seq == 0, OUTSIDE, left)
    right = jnp.where(seq == 127, OUTSIDE, right)
    row3 = jnp.concatenate([left, toks[0], right], axis=1)
    wins[0] = pltpu.roll(row3, 3 * ROWS - 124, 1)[:, :256]
    s_win = [
        send(wins.at[0], wins.at[4 * dc + d], across(d, 0, dc))
        for d, dc in ((2, 0), (2, 1), (1, 0), (3, 0), (1, 1), (3, 1), (0, 1))
    ]

    letter = lax.broadcasted_iota(I32, (8, ROWS), 0)

    def one_hots(b):
        win = wins[b]
        for i in range(9):
            ids = win[:, :ROWS] if i == 0 else pltpu.roll(win, 256 - i, 1)[:, :ROWS]
            ohf[8 * i : 8 * i + 8, :ROWS] = jnp.where(ids == letter, 1.0, 0.0)
            turned = jnp.where(ids == OUTSIDE, OUTSIDE, 3 - ids)
            ohf[64 - 8 * i : 72 - 8 * i, ROWS:] = jnp.where(turned == letter, 1.0, 0.0)
        ohb[:, 256 * b : 256 * b + 256] = ohf[...].astype(BF16)

    one_hots(0)
    for k in range(TAPS):
        hots[:, 256 * k : 256 * k + 256] = ohf[8 * k : 8 * k + 40, :].astype(BF16)

    def own_tap(k):
        hot = hots[:, 256 * k : 256 * k + 256]
        stm[...] = dot(hot, w40b[0:40, :], ((0,), (0,)))
        if k == 2:
            mine = pl.ds(pl.multiple_of(chan * HALF, 128), HALF)
            rown[0:ROWS, :] = rounded(stm[0:ROWS, mine]) + rounded(stm[ROWS:, mine])

        def strip(n, _):
            top = pl.ds(pl.multiple_of(n * 32, 32), 32)
            for c in range(0, FULL, 256):
                cols = slice(c, c + 256)
                wide = slice(FULL * k + c, FULL * k + c + 256)
                grad = grow[top, wide]
                total = None
                for side in range(2):
                    v = rounded(stm[pl.ds(pl.multiple_of(n * 32 + ROWS * side, 32), 32), cols])
                    v2 = v * v
                    h = gelu_half(v, v2)
                    act = v * h
                    total = act if total is None else total + act
                    slope = h + (act - act * h) * (2.0 * C0 + 6.0 * C1 * v2)
                    into = pl.ds(pl.multiple_of(n * 32 + 256 * k + ROWS * side, 32), 32)
                    dsb[into, cols] = (grad * slope).astype(BF16)
                skb[top, wide] = total.astype(BF16)
            return 0

        lax.fori_loop(0, ROWS // 32, strip, 0)

    own_tap(0)
    own_tap(1)
    halves = []
    for d, half in ((1, 0), (3, 1)):
        g_x[d].wait_recv()
        rows = pl.ds(64 * half, 64)
        for dc in range(2):
            into = gall.at[2 + 4 * dc, rows]
            halves.append(send(gall.at[d, rows], into, across(d, 0, dc)))
        g_sib[d] = send(gall.at[d], gall.at[4 + d], sibling)
    for k in range(2, TAPS):
        own_tap(k)

    gsacc = dot(hots[...], dsb[...], ((1,), (0,)))
    for h in range(2):
        for j in range(TAPS):
            for t in range(3):
                c = HALF * h + 128 * t
                gsend[h, 3 * j + t] = gsacc[8 * j : 8 * j + 8, c : c + 128]
        gsend[h, 15] = jnp.zeros((8, 128), F32)
    s_z = []
    for d, other in z_steps:
        part = gsend.at[1 - chan if other else chan, pl.ds(2 * lax.rem(z + d, NZ), 2)]
        s_z.append(send(part, grz.at[8 * other + d], z_by(d, other)))

    def blocks(first):
        here = slice(256 * first, 256 * first + 1024)
        stt[...] = dot(sel_ref[...], ohb[:, here], ((1,), (0,)))

        def strip(n, _):
            rows = pl.ds(pl.multiple_of(n * 64, 64), 64)
            for b in range(4):
                v = rounded(stt[rows, 256 * b : 256 * b + 256])
                act = v * gelu_half(v, v * v)
                into = slice((first + b) * ROWS, (first + b + 1) * ROWS)
                st[rows, into] = (act[:, :ROWS] + act[:, ROWS:]).astype(BF16)
            return 0

        lax.fori_loop(0, 512 // 64, strip, 0)

    for copy in s_win:
        copy.wait_recv()
    for b in range(1, 8):
        one_hots(b)
    blocks(0)
    blocks(4)
    for copy in halves + list(g_sib.values()):
        copy.wait_recv()
    every = gall[...].reshape(8 * ROWS, HALF)
    s_y = []
    for n in range(4):
        rows = slice(64 * n, 64 * n + 64)
        rsend[rows, :] = dot(st[rows, :], every, ((1,), (0,))).astype(BF16)
        s_y.append(send(rsend.at[pl.ds(64 * n, 64)], ry.at[pl.ds(64 * n, 64)], beside_y))
    for copy in s_z:
        copy.wait_recv()
    part = gsend[chan, pl.ds(2 * z, 2)]
    for d, other in z_steps:
        part = part + grz[8 * other + d]
    gone[...] = part
    me = 4 * x + 2 * y + core
    grx[me] = part
    s_gx = [send(gone, grx.at[me], across(*s)) for s in shifts]

    conv = rown[0:ROWS, :]
    conv += dot(skb[...], w_ref[...].reshape(TAPS * FULL, HALF), ((1,), (0,)))
    bl_ref[...] = (0.5 * conv).astype(BF16)
    rown[...] = dot(st[256:, :], every, ((1,), (0,)))

    s_rz = []
    for n in range(4):
        s_y[n].wait_recv()
        if n == 3:
            for copy in s_gx:
                copy.wait_recv()
            parts = [grx[n] for n in range(16)]
            while len(parts) > 1:
                parts = [p + q for p, q in zip(parts[0::2], parts[1::2])]
            gfin[pl.ds(2 * z, 2)] = 0.5 * parts[0]
            s_gf = [
                send(gfin.at[pl.ds(2 * z, 2)], gfin.at[pl.ds(2 * z, 2)], z_by(d)) for d in range(1, NZ)
            ]
        rows = slice(64 * n, 64 * n + 64)
        both = rown[rows, :] + ry[rows, :].astype(F32)
        if n == 3:
            rown[rows, :] = both
        zsend[rows, :] = both.astype(BF16)
        for m in (2 * n, 2 * n + 1):
            d = FAR_FIRST[m]
            if d:
                s_rz.append(send(zsend.at[pl.ds(32 * m, 32)], zrecv.at[d], z_by(d)))

    for copy in s_rz:
        copy.wait_recv()
    total = rown[224:256, :]
    for d in range(1, NZ):
        total = total + zrecv[d].astype(F32)
    total = 0.5 * total
    for k in range(TAPS):
        gc_ref[k] = total[6 * k : 6 * k + 6, :]
    for copy in s_gf:
        copy.wait_recv()
    for j in range(TAPS):
        for t in range(3):
            gs_ref[j, :, 128 * t : 128 * t + 128] = gfin[3 * j + t, 0:4, :]
    for copy in used:
        copy.wait_send()


def on_device(tokens, stem_weight, conv_weight, cotangent):
    vmem = pl.BlockSpec(memory_space=pltpu.VMEM)
    hbm = pl.BlockSpec(memory_space=pltpu.HBM)
    V = pltpu.VMEM
    return pl.pallas_call(
        kernel,
        out_shape=(
            jax.ShapeDtypeStruct((ROWS, HALF), BF16),
            jax.ShapeDtypeStruct((TAPS, 6, HALF), F32),
            jax.ShapeDtypeStruct((TAPS, 4, HALF), F32),
        ),
        in_specs=[hbm, hbm, hbm, hbm],
        out_specs=(vmem, vmem, vmem),
        scratch_shapes=[
            V((TAPS, FULL, HALF), BF16), V((1, ROWS), I32), V((TAPS, 4, FULL), BF16),
            V((3, 8, ROWS), I32), V((8, 8, 256), I32),
            V((8, ROWS, HALF), BF16), V((128, FULL), F32), V((128, FULL), BF16),
            V((512, 128), BF16), V((128, 256), F32), V((128, 2048), BF16), V((40, 1280), BF16),
            V((256, FULL), F32), V((ROWS, TAPS * FULL), F32),
            V((ROWS, TAPS * FULL), BF16), V((TAPS * 256, FULL), BF16),
            V((512, 1024), F32), V((512, 1024), BF16), V((256, HALF), BF16),
            V((256, HALF), F32), V((256, HALF), BF16), V((256, HALF), BF16), V((8, 32, HALF), BF16),
            V((2, 16, 8, 128), F32), V((16, 2, 8, 128), F32),
            V((2, 8, 128), F32), V((16, 2, 8, 128), F32), V((16, 8, 128), F32),
            pltpu.SemaphoreType.DMA((8,)), pltpu.SemaphoreType.DMA((80,)),
            pltpu.SemaphoreType.DMA((80,)),
        ],
        compiler_params=pltpu.CompilerParams(
            collective_id=0, has_side_effects=True, vmem_limit_bytes=48 * 2**20
        ),
    )(tokens.reshape(1, ROWS), stem_weight, conv_weight, cotangent)


def solution(mesh):
    return jax.shard_map(
        on_device,
        mesh=mesh,
        in_specs=(P("seq"), P(), P(None, None, "chan"), P("seq", "chan")),
        out_specs=(P("seq", "chan"), P(None, "seq", "chan"), P(None, None, "chan")),
        check_vma=False,
    )
```

```python
import math

import jax
import jax.numpy as jnp
from jax import lax
from jax.experimental import pallas as pl
from jax.experimental.pallas import tpu as pltpu
from jax.sharding import PartitionSpec as P

F32, BF16, I32 = jnp.float32, jnp.bfloat16, jnp.int32
C0 = math.sqrt(2.0 / math.pi)
C1 = C0 * 0.044715
OUTSIDE = 4
FAR_FIRST = (4, 3, 5, 2, 6, 1, 7, 0)
ROWS, FULL, HALF, TAPS = 128, 768, 384, 5
NX, NY, NZ = 4, 2, 8


def dot(a, b, dims):
    return lax.dot_general(a, b, (dims, ((), ())), preferred_element_type=F32)


def f32(v):
    return v.astype(F32)


def gelu_half(v, v2):
    return 0.5 + 0.5 * jnp.tanh(v * (C0 + C1 * v2))


def kernel(
    tok_hbm, sw_hbm, w_hbm, cot_hbm,
    bl_ref, gc_ref, gs_ref,
    w_ref, tok_ref, sw_ref, toks, wins, gall, w40, w40b, sel_ref, ohf, ohb, hots, stm, grow, skb, dsb,
    stt, st, rsend, rown, ry, zsend, zrecv,
    gsend, grz, gone, grx, gfin,
    wsem, ssem, rsem,
):
    seq, chan = lax.axis_index("seq"), lax.axis_index("chan")
    core = lax.rem(seq, 2)
    z = lax.rem(lax.div(seq, 2), NZ)
    y = lax.rem(lax.div(seq, 2 * NZ), NY)
    x = lax.div(seq, 2 * NZ * NY)

    def at(px, py, pz, pc, ch):
        return (((px * NY + py) * NZ + pz) * 2 + pc, ch)

    def x_by(d):
        return at(lax.rem(x + d, NX), y, z, core, chan)

    def z_by(d):
        return at(x, y, lax.rem(z + d, NZ), core, chan)

    def across(dx, dy, dc, dh=0):
        return at(
            lax.rem(x + dx, NX), 1 - y if dy else y, z, 1 - core if dc else core,
            1 - chan if dh else chan,
        )

    sibling = across(0, 0, 1)
    beside_y = across(0, 1, 0)
    outer = (lax.rem(seq + 128 + 2 * core - 1, 128), chan)
    shifts = [
        (dx, dy, dc, dh) for dh in (1, 0) for dy in (1, 0) for dx in (2, 1, 3, 0) for dc in (1, 0)
    ][:-1]
    partners = [outer] + [across(*s) for s in shifts] + [z_by(d) for d in FAR_FIRST[:-1]]

    barrier = pltpu.get_barrier_semaphore()
    for device in partners:
        pl.semaphore_signal(
            barrier, inc=1, device_id=device, device_id_type=pl.DeviceIdType.MESH
        )

    used = []

    def send(src, dst, device):
        n = len(used)
        copy = pltpu.make_async_remote_copy(
            src_ref=src, dst_ref=dst, send_sem=ssem.at[n], recv_sem=rsem.at[n],
            device_id=device, device_id_type=pl.DeviceIdType.MESH,
        )
        copy.start()
        used.append(copy)
        return copy

    def load(n, src, dst):
        copy = pltpu.make_async_copy(src, dst, wsem.at[n])
        copy.start()
        return copy

    load_tok = load(5, tok_hbm, tok_ref)
    load_sw = load(6, sw_hbm, sw_ref)
    load_cot = load(7, cot_hbm, gall.at[0])
    loads = [load(k, w_hbm.at[k], w_ref.at[k]) for k in range(TAPS)]

    w40[...] = jnp.zeros_like(w40)
    ohf[...] = jnp.zeros_like(ohf)
    pl.semaphore_wait(barrier, len(partners))

    tok_out = send(tok_hbm, toks.at[1], outer)
    tok_sib = send(tok_hbm, toks.at[0], sibling)
    g_x = {d: send(cot_hbm, gall.at[d], x_by(d)) for d in (1, 3)}
    g_sib = {0: send(cot_hbm, gall.at[4], sibling)}

    load_sw.wait()
    for j in range(TAPS):
        w40[8 * j : 8 * j + 4, :] = sw_ref[j].astype(F32)
    w40[20:21, :] = jnp.full((1, FULL), -128.0, F32)
    w40b[...] = w40[...].astype(BF16)

    row = lax.broadcasted_iota(I32, (512, 1), 0)
    rest = row & 31
    tap = (rest * 43) >> 8
    place = (row >> 5) & 7
    step = jnp.zeros_like(row)
    for n, d in enumerate(FAR_FIRST):
        step = jnp.where(place == n, d, step)
    zrow = (z + step) & 7
    yrow = jnp.where(row < 256, 1 - y, y)
    col = 192 * x + 96 * yrow + 12 * zrow + 6 * core + rest - 6 * tap
    col = jnp.where(tap < TAPS, col, -1)
    lane = lax.broadcasted_iota(I32, (512, FULL), 1)
    chosen = jnp.where(lane == col, 1.0, 0.0).astype(BF16)
    table = dot(chosen, w40b[...], ((1,), (1,)))
    placed = jnp.zeros((512, 128), F32)
    for k in range(TAPS):
        moved = table if k == 0 else pltpu.roll(table, 8 * k, 1)
        placed = jnp.where(tap == k, moved, placed)
    sel_ref[...] = placed.astype(BF16)

    load_cot.wait()
    for k in range(TAPS):
        loads[k].wait()
        grow[:, FULL * k : FULL * (k + 1)] = dot(gall[0], w_ref[k], ((1,), (1,)))

    load_tok.wait()
    tok_sib.wait_recv()
    tok_out.wait_recv()
    near = jnp.broadcast_to(toks[0], (8, ROWS))
    far = jnp.broadcast_to(toks[1], (8, ROWS))
    own = jnp.broadcast_to(tok_ref[...], (8, ROWS))
    left = jnp.where(core == 1, near, far)
    right = jnp.where(core == 1, far, near)
    left = jnp.where(seq == 0, OUTSIDE, left)
    right = jnp.where(seq == 127, OUTSIDE, right)
    row3 = jnp.concatenate([left, own, right], axis=1)
    wins[0] = pltpu.roll(row3, 3 * ROWS - 124, 1)[:, :256]
    s_win = [
        send(wins.at[0], wins.at[4 * dc + d], across(d, 0, dc))
        for d, dc in ((2, 0), (2, 1), (1, 0), (3, 0), (1, 1), (3, 1), (0, 1))
    ]

    letter = lax.broadcasted_iota(I32, (8, ROWS), 0)

    def one_hots(b):
        win = wins[b]
        for i in range(9):
            ids = win[:, :ROWS] if i == 0 else pltpu.roll(win, 256 - i, 1)[:, :ROWS]
            ohf[8 * i : 8 * i + 8, :ROWS] = jnp.where(ids == letter, 1.0, 0.0)
            turned = jnp.where(ids == OUTSIDE, OUTSIDE, 3 - ids)
            ohf[64 - 8 * i : 72 - 8 * i, ROWS:] = jnp.where(turned == letter, 1.0, 0.0)
        ohb[:, 256 * b : 256 * b + 256] = ohf[...].astype(BF16)

    one_hots(0)
    for k in range(TAPS):
        hots[:, 256 * k : 256 * k + 256] = ohf[8 * k : 8 * k + 40, :].astype(BF16)

    def own_tap(k):
        hot = hots[:, 256 * k : 256 * k + 256]
        stm[...] = dot(hot, w40b[0:40, :], ((0,), (0,))).astype(BF16)
        if k == 2:
            half = pl.ds(pl.multiple_of(chan * HALF, 128), HALF)
            rown[0:ROWS, :] = f32(stm[0:ROWS, half]) + f32(stm[ROWS:, half])

        def strip(n, _):
            top = pl.ds(pl.multiple_of(n * 32, 32), 32)
            for c in range(0, FULL, 256):
                cols = slice(c, c + 256)
                wide = slice(FULL * k + c, FULL * k + c + 256)
                grad = grow[top, wide]
                total = None
                for side in range(2):
                    v = f32(stm[pl.ds(pl.multiple_of(n * 32 + ROWS * side, 32), 32), cols])
                    v2 = v * v
                    h = gelu_half(v, v2)
                    act = v * h
                    total = act if total is None else total + act
                    slope = h + (act - act * h) * (2.0 * C0 + 6.0 * C1 * v2)
                    into = pl.ds(pl.multiple_of(n * 32 + 256 * k + ROWS * side, 32), 32)
                    dsb[into, cols] = (grad * slope).astype(BF16)
                skb[top, wide] = total.astype(BF16)
            return 0

        lax.fori_loop(0, ROWS // 32, strip, 0, unroll=True)

    own_tap(0)
    own_tap(1)
    halves = []
    for d, half in ((1, 0), (3, 1)):
        g_x[d].wait_recv()
        rows = pl.ds(64 * half, 64)
        for dc in range(2):
            into = gall.at[2 + 4 * dc, rows]
            halves.append(send(gall.at[d, rows], into, across(d, 0, dc)))
        g_sib[d] = send(gall.at[d], gall.at[4 + d], sibling)
    for k in range(2, TAPS):
        own_tap(k)

    gsacc = dot(hots[...], dsb[...], ((1,), (0,)))
    for h in range(2):
        for j in range(TAPS):
            for t in range(3):
                c = HALF * h + 128 * t
                gsend[h, 3 * j + t] = gsacc[8 * j : 8 * j + 8, c : c + 128]
        gsend[h, 15] = jnp.zeros((8, 128), F32)
    mine = 2 * x + core
    me = 8 * chan + 4 * y + x + 16 * core
    grz[me] = gsend[chan, pl.ds(2 * mine, 2)]
    s_z = []
    for dx, dy, dc, dh in shifts:
        owner = 2 * lax.rem(x + dx, NX) + (1 - core if dc else core)
        part = gsend.at[1 - chan if dh else chan, pl.ds(2 * owner, 2)]
        s_z.append(send(part, grz.at[me], across(dx, dy, dc, dh)))

    def blocks(first):
        here = slice(256 * first, 256 * first + 1024)
        stt[...] = dot(sel_ref[...], ohb[:, here], ((1,), (0,))).astype(BF16)

        def strip(n, _):
            rows = pl.ds(pl.multiple_of(n * 64, 64), 64)
            for b in range(4):
                v = f32(stt[rows, 256 * b : 256 * b + 256])
                act = v * gelu_half(v, v * v)
                into = slice((first + b) * ROWS, (first + b + 1) * ROWS)
                st[rows, into] = (act[:, :ROWS] + act[:, ROWS:]).astype(BF16)
            return 0

        lax.fori_loop(0, 512 // 64, strip, 0, unroll=True)

    for copy in s_win:
        copy.wait_recv()
    for b in range(1, 8):
        one_hots(b)
    blocks(0)
    blocks(4)
    for copy in halves + list(g_sib.values()):
        copy.wait_recv()
    every = gall[...].reshape(8 * ROWS, HALF)
    s_y = []
    for n in range(4):
        rows = slice(64 * n, 64 * n + 64)
        rsend[rows, :] = dot(st[rows, :], every, ((1,), (0,))).astype(BF16)
        s_y.append(send(rsend.at[pl.ds(64 * n, 64)], ry.at[pl.ds(64 * n, 64)], beside_y))
    for copy in s_z:
        copy.wait_recv()
    part = grz[0]
    for n in range(1, 32):
        part = part + grz[n]
    gone[...] = part
    grx[z] = part
    s_gx = [send(gone, grx.at[z], z_by(d)) for d in FAR_FIRST[:-1]]

    conv = rown[0:ROWS, :]
    conv += dot(skb[...], w_ref[...].reshape(TAPS * FULL, HALF), ((1,), (0,)))
    bl_ref[...] = (0.5 * conv).astype(BF16)
    rown[...] = dot(st[256:, :], every, ((1,), (0,)))

    s_rz = []
    for n in range(4):
        s_y[n].wait_recv()
        rows = slice(64 * n, 64 * n + 64)
        both = rown[rows, :] + ry[rows, :].astype(F32)
        if n == 3:
            rown[rows, :] = both
        zsend[rows, :] = both.astype(BF16)
        for m in (2 * n, 2 * n + 1):
            d = FAR_FIRST[m]
            if d:
                s_rz.append(send(zsend.at[pl.ds(32 * m, 32)], zrecv.at[d], z_by(d)))


    for copy in s_gx:
        copy.wait_recv()
    parts = [grx[m] for m in range(NZ)]
    while len(parts) > 1:
        parts = [p + q for p, q in zip(parts[0::2], parts[1::2])]
    whole = gfin.at[pl.ds(2 * mine, 2)]
    whole[...] = 0.5 * parts[0]
    s_gf = [
        send(whole, whole, across(dx, 0, dc))
        for dx, dc in ((2, 1), (2, 0), (1, 1), (3, 1), (1, 0), (3, 0), (0, 1))
    ]

    for copy in s_rz:
        copy.wait_recv()
    total = rown[224:256, :]
    for d in range(1, NZ):
        total = total + zrecv[d].astype(F32)
    total = 0.5 * total
    for k in range(TAPS):
        gc_ref[k] = total[6 * k : 6 * k + 6, :]
    for copy in s_gf:
        copy.wait_recv()
    for j in range(TAPS):
        for t in range(3):
            gs_ref[j, :, 128 * t : 128 * t + 128] = gfin[3 * j + t, 0:4, :]
    for copy in used:
        copy.wait_send()


def on_device(tokens, stem_weight, conv_weight, cotangent):
    vmem = pl.BlockSpec(memory_space=pltpu.VMEM)
    hbm = pl.BlockSpec(memory_space=pltpu.HBM)
    V = pltpu.VMEM
    return pl.pallas_call(
        kernel,
        out_shape=(
            jax.ShapeDtypeStruct((ROWS, HALF), BF16),
            jax.ShapeDtypeStruct((TAPS, 6, HALF), F32),
            jax.ShapeDtypeStruct((TAPS, 4, HALF), F32),
        ),
        in_specs=[hbm, hbm, hbm, hbm],
        out_specs=(vmem, vmem, vmem),
        scratch_shapes=[
            V((TAPS, FULL, HALF), BF16), V((1, ROWS), I32), V((TAPS, 4, FULL), BF16),
            V((2, 1, ROWS), I32), V((8, 8, 256), I32),
            V((8, ROWS, HALF), BF16), V((128, FULL), F32), V((128, FULL), BF16),
            V((512, 128), BF16), V((128, 256), F32), V((128, 2048), BF16), V((40, 1280), BF16),
            V((256, FULL), BF16), V((ROWS, TAPS * FULL), F32),
            V((ROWS, TAPS * FULL), BF16), V((TAPS * 256, FULL), BF16),
            V((512, 1024), BF16), V((512, 1024), BF16), V((256, HALF), BF16),
            V((256, HALF), F32), V((256, HALF), BF16), V((256, HALF), BF16), V((8, 32, HALF), BF16),
            V((2, 16, 8, 128), F32), V((32, 2, 8, 128), F32),
            V((2, 8, 128), F32), V((NZ, 2, 8, 128), F32), V((16, 8, 128), F32),
            pltpu.SemaphoreType.DMA((8,)), pltpu.SemaphoreType.DMA((96,)),
            pltpu.SemaphoreType.DMA((96,)),
        ],
        compiler_params=pltpu.CompilerParams(
            collective_id=0, has_side_effects=True, vmem_limit_bytes=48 * 2**20
        ),
    )(tokens.reshape(1, ROWS), stem_weight, conv_weight, cotangent)


def solution(mesh):
    return jax.shard_map(
        on_device,
        mesh=mesh,
        in_specs=(P("seq"), P(), P(None, None, "chan"), P("seq", "chan")),
        out_specs=(P("seq", "chan"), P(None, "seq", "chan"), P(None, None, "chan")),
        check_vma=False,
    )
```

```python
import math

import jax
import jax.numpy as jnp
from jax import lax
from jax.experimental import pallas as pl
from jax.experimental.pallas import tpu as pltpu
from jax.sharding import PartitionSpec as P

F32, BF16, I32 = jnp.float32, jnp.bfloat16, jnp.int32
C0 = math.sqrt(2.0 / math.pi)
C1 = C0 * 0.044715
OUTSIDE = 4
FAR_FIRST = (4, 3, 5, 2, 6, 1, 7, 0)
CHUNKS = ((0, 2), (2, 4), (4, 7), (7, 8))
ROWS, FULL, HALF, TAPS = 128, 768, 384, 5
NX, NY, NZ = 4, 2, 8


def dot(a, b, dims):
    return lax.dot_general(a, b, (dims, ((), ())), preferred_element_type=F32)


def f32(v):
    return v.astype(F32)


def gelu_half(v, v2):
    return 0.5 + 0.5 * jnp.tanh(v * (C0 + C1 * v2))


def kernel(
    tok_hbm, sw_hbm, w_hbm, cot_hbm,
    bl_ref, gc_ref, gs_ref,
    w_ref, tok_ref, sw_ref, toks, wins, gall, w40, w40b, sel_ref, ohf, ohb, hots, stm, grow, skb, dsb,
    stt, st, rsend, rown, ry, zsend, zrecv,
    gsend, grz, gone, grx, gfin,
    wsem, ssem, rsem,
):
    seq, chan = lax.axis_index("seq"), lax.axis_index("chan")
    core = lax.rem(seq, 2)
    z = lax.rem(lax.div(seq, 2), NZ)
    y = lax.rem(lax.div(seq, 2 * NZ), NY)
    x = lax.div(seq, 2 * NZ * NY)

    def at(px, py, pz, pc, ch):
        return (((px * NY + py) * NZ + pz) * 2 + pc, ch)

    def x_by(d):
        return at(lax.rem(x + d, NX), y, z, core, chan)

    def z_by(d):
        return at(x, y, lax.rem(z + d, NZ), core, chan)

    def across(dx, dy, dc, dh=0):
        return at(
            lax.rem(x + dx, NX), 1 - y if dy else y, z, 1 - core if dc else core,
            1 - chan if dh else chan,
        )

    sibling = across(0, 0, 1)
    beside_y = across(0, 1, 0)
    outer = (lax.rem(seq + 128 + 2 * core - 1, 128), chan)
    cores = [(dx, dc) for dx in (2, 1, 3, 0) for dc in (1, 0)]
    halves_of = [(dx, 0, dc, dh) for dh in (1, 0) for dx, dc in cores][:-1]
    sides_of = [(dx, dy, dc) for dy in (1, 0) for dx, dc in cores][:-1]
    partners = [outer] + [across(*s) for s in halves_of] + [across(*s) for s in sides_of[:8]]
    partners += [z_by(d) for d in FAR_FIRST[:-1]]

    barrier = pltpu.get_barrier_semaphore()
    for device in partners:
        pl.semaphore_signal(
            barrier, inc=1, device_id=device, device_id_type=pl.DeviceIdType.MESH
        )

    used = []

    def send(src, dst, device):
        n = len(used)
        copy = pltpu.make_async_remote_copy(
            src_ref=src, dst_ref=dst, send_sem=ssem.at[n], recv_sem=rsem.at[n],
            device_id=device, device_id_type=pl.DeviceIdType.MESH,
        )
        copy.start()
        used.append(copy)
        return copy

    def load(n, src, dst):
        copy = pltpu.make_async_copy(src, dst, wsem.at[n])
        copy.start()
        return copy

    load_tok = load(5, tok_hbm, tok_ref)
    load_sw = load(6, sw_hbm, sw_ref)
    load_cot = load(7, cot_hbm, gall.at[0])
    loads = [load(k, w_hbm.at[k], w_ref.at[k]) for k in range(TAPS)]

    w40[...] = jnp.zeros_like(w40)
    ohf[...] = jnp.zeros_like(ohf)
    pl.semaphore_wait(barrier, len(partners))

    tok_out = send(tok_hbm, toks.at[1], outer)
    tok_sib = send(tok_hbm, toks.at[0], sibling)
    g_x = {d: send(cot_hbm, gall.at[d], x_by(d)) for d in (1, 3)}
    g_sib = {0: send(cot_hbm, gall.at[4], sibling)}

    load_sw.wait()
    for j in range(TAPS):
        w40[8 * j : 8 * j + 4, :] = sw_ref[j].astype(F32)
    w40[20:21, :] = jnp.full((1, FULL), -128.0, F32)
    w40b[...] = w40[...].astype(BF16)

    row = lax.broadcasted_iota(I32, (512, 1), 0)
    rest = row & 31
    tap = (rest * 43) >> 8
    place = (row >> 5) & 7
    step = jnp.zeros_like(row)
    for n, d in enumerate(FAR_FIRST):
        step = jnp.where(place == n, d, step)
    zrow = (z + step) & 7
    yrow = jnp.where(row < 256, 1 - y, y)
    col = 192 * x + 96 * yrow + 12 * zrow + 6 * core + rest - 6 * tap
    col = jnp.where(tap < TAPS, col, -1)
    lane = lax.broadcasted_iota(I32, (512, FULL), 1)
    chosen = jnp.where(lane == col, 1.0, 0.0).astype(BF16)
    table = dot(chosen, w40b[...], ((1,), (1,)))
    placed = jnp.zeros((512, 128), F32)
    for k in range(TAPS):
        moved = table if k == 0 else pltpu.roll(table, 8 * k, 1)
        placed = jnp.where(tap == k, moved, placed)
    sel_ref[...] = placed.astype(BF16)

    load_cot.wait()
    for k in range(TAPS):
        loads[k].wait()
        grow[:, FULL * k : FULL * (k + 1)] = dot(gall[0], w_ref[k], ((1,), (1,)))

    load_tok.wait()
    tok_sib.wait_recv()
    tok_out.wait_recv()
    near = jnp.broadcast_to(toks[0], (8, ROWS))
    far = jnp.broadcast_to(toks[1], (8, ROWS))
    own = jnp.broadcast_to(tok_ref[...], (8, ROWS))
    left = jnp.where(core == 1, near, far)
    right = jnp.where(core == 1, far, near)
    left = jnp.where(seq == 0, OUTSIDE, left)
    right = jnp.where(seq == 127, OUTSIDE, right)
    row3 = jnp.concatenate([left, own, right], axis=1)
    wins[0] = pltpu.roll(row3, 3 * ROWS - 124, 1)[:, :256]
    letter = lax.broadcasted_iota(I32, (8, ROWS), 0)

    def one_hots(b):
        win = wins[b]
        for i in range(9):
            ids = win[:, :ROWS] if i == 0 else pltpu.roll(win, 256 - i, 1)[:, :ROWS]
            ohf[8 * i : 8 * i + 8, :ROWS] = jnp.where(ids == letter, 1.0, 0.0)
            turned = jnp.where(ids == OUTSIDE, OUTSIDE, 3 - ids)
            ohf[64 - 8 * i : 72 - 8 * i, ROWS:] = jnp.where(turned == letter, 1.0, 0.0)
        ohb[:, 256 * b : 256 * b + 256] = ohf[...].astype(BF16)

    one_hots(0)
    for k in range(TAPS):
        hots[:, 256 * k : 256 * k + 256] = ohf[8 * k : 8 * k + 40, :].astype(BF16)

    def own_tap(k):
        hot = hots[:, 256 * k : 256 * k + 256]
        stm[...] = dot(hot, w40b[0:40, :], ((0,), (0,))).astype(BF16)
        if k == 2:
            half = pl.ds(pl.multiple_of(chan * HALF, 128), HALF)
            rown[0:ROWS, :] = f32(stm[0:ROWS, half]) + f32(stm[ROWS:, half])

        def strip(n, _):
            top = pl.ds(pl.multiple_of(n * 32, 32), 32)
            for c in range(0, FULL, 256):
                cols = slice(c, c + 256)
                wide = slice(FULL * k + c, FULL * k + c + 256)
                grad = grow[top, wide]
                total = None
                for side in range(2):
                    v = f32(stm[pl.ds(pl.multiple_of(n * 32 + ROWS * side, 32), 32), cols])
                    v2 = v * v
                    h = gelu_half(v, v2)
                    act = v * h
                    total = act if total is None else total + act
                    slope = h + (act - act * h) * (2.0 * C0 + 6.0 * C1 * v2)
                    into = pl.ds(pl.multiple_of(n * 32 + 256 * k + ROWS * side, 32), 32)
                    dsb[into, cols] = (grad * slope).astype(BF16)
                skb[top, wide] = total.astype(BF16)
            return 0

        lax.fori_loop(0, ROWS // 32, strip, 0, unroll=True)

    own_tap(0)
    s_win = [
        send(wins.at[0], wins.at[4 * dc + d], across(d, 0, dc))
        for d, dc in ((2, 0), (2, 1), (1, 0), (3, 0), (1, 1), (3, 1), (0, 1))
    ]
    own_tap(1)
    halves = []
    for d, half in ((1, 0), (3, 1)):
        g_x[d].wait_recv()
        rows = pl.ds(64 * half, 64)
        for dc in range(2):
            into = gall.at[2 + 4 * dc, rows]
            halves.append(send(gall.at[d, rows], into, across(d, 0, dc)))
        g_sib[d] = send(gall.at[d], gall.at[4 + d], sibling)
    for k in range(2, TAPS):
        own_tap(k)

    gsacc = dot(hots[...], dsb[...], ((1,), (0,)))
    for h in range(2):
        for j in range(TAPS):
            for t in range(3):
                c = HALF * h + 128 * t
                gsend[h, 3 * j + t] = gsacc[8 * j : 8 * j + 8, c : c + 128]
        gsend[h, 15] = jnp.zeros((8, 128), F32)
    mine = 2 * x + core
    me = 8 * chan + 4 * core + x
    grz[me] = gsend[chan, pl.ds(2 * mine, 2)]
    s_z = []
    for dx, dy, dc, dh in halves_of:
        owner = 2 * lax.rem(x + dx, NX) + (1 - core if dc else core)
        part = gsend.at[1 - chan if dh else chan, pl.ds(2 * owner, 2)]
        s_z.append(send(part, grz.at[me], across(dx, dy, dc, dh)))

    def blocks(first):
        here = slice(256 * first, 256 * first + 1024)
        stt[...] = dot(sel_ref[...], ohb[:, here], ((1,), (0,))).astype(BF16)

        def strip(n, _):
            rows = pl.ds(pl.multiple_of(n * 64, 64), 64)
            for b in range(4):
                v = f32(stt[rows, 256 * b : 256 * b + 256])
                act = v * gelu_half(v, v * v)
                into = slice((first + b) * ROWS, (first + b + 1) * ROWS)
                st[rows, into] = (act[:, :ROWS] + act[:, ROWS:]).astype(BF16)
            return 0

        lax.fori_loop(0, 512 // 64, strip, 0, unroll=True)

    for copy in s_win:
        copy.wait_recv()
    for b in range(1, 8):
        one_hots(b)
    blocks(0)
    blocks(4)
    for copy in halves + list(g_sib.values()):
        copy.wait_recv()
    every = gall[...].reshape(8 * ROWS, HALF)
    s_y = []
    for n, (first, last) in enumerate(CHUNKS):
        rows = slice(32 * first, 32 * last)
        span = pl.ds(32 * first, 32 * (last - first))
        rsend[rows, :] = dot(st[rows, :], every, ((1,), (0,))).astype(BF16)
        s_y.append(send(rsend.at[span], ry.at[span], beside_y))
    for copy in s_z:
        copy.wait_recv()
    part = grz[0]
    for n in range(1, 16):
        part = part + grz[n]
    gone[...] = part
    grx[z] = part
    s_gx = [send(gone, grx.at[z], z_by(d)) for d in FAR_FIRST[:-1]]

    conv = rown[0:ROWS, :]
    conv += dot(skb[...], w_ref[...].reshape(TAPS * FULL, HALF), ((1,), (0,)))
    bl_ref[...] = (0.5 * conv).astype(BF16)
    rown[...] = dot(st[256:, :], every, ((1,), (0,)))

    s_rz = []
    for n, (first, last) in enumerate(CHUNKS):
        if n == 3:
            for copy in s_gx:
                copy.wait_recv()
            parts = [grx[m] for m in range(NZ)]
            while len(parts) > 1:
                parts = [p + q for p, q in zip(parts[0::2], parts[1::2])]
            whole = gfin.at[y, pl.ds(2 * mine, 2)]
            whole[...] = 0.5 * parts[0]
            s_gf = [send(whole, whole, across(*s)) for s in sides_of]
        s_y[n].wait_recv()
        rows = slice(32 * first, 32 * last)
        both = rown[rows, :] + ry[rows, :].astype(F32)
        if n == 3:
            rown[rows, :] = both
        zsend[rows, :] = both.astype(BF16)
        for m in range(first, last):
            d = FAR_FIRST[m]
            if d:
                s_rz.append(send(zsend.at[pl.ds(32 * m, 32)], zrecv.at[d], z_by(d)))


    for copy in s_rz:
        copy.wait_recv()
    total = rown[224:256, :]
    for d in range(1, NZ):
        total = total + zrecv[d].astype(F32)
    total = 0.5 * total
    for k in range(TAPS):
        gc_ref[k] = total[6 * k : 6 * k + 6, :]
    for copy in s_gf:
        copy.wait_recv()
    for j in range(TAPS):
        for t in range(3):
            gs_ref[j, :, 128 * t : 128 * t + 128] = gfin[0, 3 * j + t, 0:4, :] + gfin[1, 3 * j + t, 0:4, :]
    for copy in used:
        copy.wait_send()


def on_device(tokens, stem_weight, conv_weight, cotangent):
    vmem = pl.BlockSpec(memory_space=pltpu.VMEM)
    hbm = pl.BlockSpec(memory_space=pltpu.HBM)
    V = pltpu.VMEM
    return pl.pallas_call(
        kernel,
        out_shape=(
            jax.ShapeDtypeStruct((ROWS, HALF), BF16),
            jax.ShapeDtypeStruct((TAPS, 6, HALF), F32),
            jax.ShapeDtypeStruct((TAPS, 4, HALF), F32),
        ),
        in_specs=[hbm, hbm, hbm, hbm],
        out_specs=(vmem, vmem, vmem),
        scratch_shapes=[
            V((TAPS, FULL, HALF), BF16), V((1, ROWS), I32), V((TAPS, 4, FULL), BF16),
            V((2, 1, ROWS), I32), V((8, 8, 256), I32),
            V((8, ROWS, HALF), BF16), V((128, FULL), F32), V((128, FULL), BF16),
            V((512, 128), BF16), V((128, 256), F32), V((128, 2048), BF16), V((40, 1280), BF16),
            V((256, FULL), BF16), V((ROWS, TAPS * FULL), F32),
            V((ROWS, TAPS * FULL), BF16), V((TAPS * 256, FULL), BF16),
            V((512, 1024), BF16), V((512, 1024), BF16), V((256, HALF), BF16),
            V((256, HALF), F32), V((256, HALF), BF16), V((256, HALF), BF16), V((8, 32, HALF), BF16),
            V((2, 16, 8, 128), F32), V((16, 2, 8, 128), F32),
            V((2, 8, 128), F32), V((NZ, 2, 8, 128), F32), V((NY, 16, 8, 128), F32),
            pltpu.SemaphoreType.DMA((8,)), pltpu.SemaphoreType.DMA((96,)),
            pltpu.SemaphoreType.DMA((96,)),
        ],
        compiler_params=pltpu.CompilerParams(
            collective_id=0, has_side_effects=True, vmem_limit_bytes=48 * 2**20
        ),
    )(tokens.reshape(1, ROWS), stem_weight, conv_weight, cotangent)


def solution(mesh):
    return jax.shard_map(
        on_device,
        mesh=mesh,
        in_specs=(P("seq"), P(), P(None, None, "chan"), P("seq", "chan")),
        out_specs=(P("seq", "chan"), P(None, "seq", "chan"), P(None, None, "chan")),
        check_vma=False,
    )
```

```python
import math

import jax
import jax.numpy as jnp
from jax import lax
from jax.experimental import pallas as pl
from jax.experimental.pallas import tpu as pltpu
from jax.sharding import PartitionSpec as P

F32, BF16, I32 = jnp.float32, jnp.bfloat16, jnp.int32
C0 = math.sqrt(2.0 / math.pi)
C1 = C0 * 0.044715
OUTSIDE = 4
FAR_FIRST = (4, 3, 5, 2, 6, 1, 7, 0)
CHUNKS = ((0, 2), (2, 4), (4, 7), (7, 8))
ROWS, FULL, HALF, TAPS = 128, 768, 384, 5
NX, NY, NZ = 4, 2, 8


def dot(a, b, dims):
    return lax.dot_general(a, b, (dims, ((), ())), preferred_element_type=F32)


def f32(v):
    return v.astype(F32)


def gelu_half(v, v2):
    return 0.5 + 0.5 * jnp.tanh(v * (C0 + C1 * v2))


def kernel(
    tok_hbm, sw_hbm, w_hbm, cot_hbm,
    bl_ref, gc_ref, gs_ref,
    w_ref, tok_ref, sw_ref, toks, wins, gall, w40, w40b, sel_ref, ohf, ohb, hots, stm, grow, skb, dsb,
    stt, st, rsend, rown, ry, zsend, zrecv,
    gsend, grz, gone, grx, gfin,
    wsem, ssem, rsem,
):
    seq, chan = lax.axis_index("seq"), lax.axis_index("chan")
    core = lax.rem(seq, 2)
    z = lax.rem(lax.div(seq, 2), NZ)
    y = lax.rem(lax.div(seq, 2 * NZ), NY)
    x = lax.div(seq, 2 * NZ * NY)

    def at(px, py, pz, pc, ch):
        return (((px * NY + py) * NZ + pz) * 2 + pc, ch)

    def x_by(d):
        return at(lax.rem(x + d, NX), y, z, core, chan)

    def z_by(d):
        return at(x, y, lax.rem(z + d, NZ), core, chan)

    def across(dx, dy, dc, dh=0):
        return at(
            lax.rem(x + dx, NX), 1 - y if dy else y, z, 1 - core if dc else core,
            1 - chan if dh else chan,
        )

    sibling = across(0, 0, 1)
    beside_y = across(0, 1, 0)
    outer = (lax.rem(seq + 128 + 2 * core - 1, 128), chan)
    cores = [(dx, dc) for dx in (2, 1, 3, 0) for dc in (1, 0)]
    halves_of = [(dx, 0, dc, dh) for dh in (1, 0) for dx, dc in cores][:-1]
    sides_of = [(dx, dy, dc) for dy in (1, 0) for dx, dc in cores][:-1]
    partners = [outer] + [across(*s) for s in halves_of] + [across(*s) for s in sides_of[:8]]
    partners += [z_by(d) for d in FAR_FIRST[:-1]]

    barrier = pltpu.get_barrier_semaphore()
    for device in partners:
        pl.semaphore_signal(
            barrier, inc=1, device_id=device, device_id_type=pl.DeviceIdType.MESH
        )

    used = []

    def send(src, dst, device):
        n = len(used)
        copy = pltpu.make_async_remote_copy(
            src_ref=src, dst_ref=dst, send_sem=ssem.at[n], recv_sem=rsem.at[n],
            device_id=device, device_id_type=pl.DeviceIdType.MESH,
        )
        copy.start()
        used.append(copy)
        return copy

    def load(n, src, dst):
        copy = pltpu.make_async_copy(src, dst, wsem.at[n])
        copy.start()
        return copy

    load_tok = load(5, tok_hbm, tok_ref)
    load_sw = load(6, sw_hbm, sw_ref)
    load_cot = load(7, cot_hbm, gall.at[0])
    loads = [load(k, w_hbm.at[k], w_ref.at[k]) for k in range(TAPS)]

    w40[...] = jnp.zeros_like(w40)
    ohf[...] = jnp.zeros_like(ohf)
    pl.semaphore_wait(barrier, len(partners))

    tok_out = send(tok_hbm, toks.at[1], outer)
    tok_sib = send(tok_hbm, toks.at[0], sibling)
    g_x = {d: send(cot_hbm, gall.at[d], x_by(d)) for d in (1, 3)}
    g_sib = {0: send(cot_hbm, gall.at[4], sibling)}

    load_sw.wait()
    for j in range(TAPS):
        w40[8 * j : 8 * j + 4, :] = sw_ref[j].astype(F32)
    w40[20:21, :] = jnp.full((1, FULL), -128.0, F32)
    w40b[...] = w40[...].astype(BF16)

    row = lax.broadcasted_iota(I32, (512, 1), 0)
    rest = row & 31
    tap = (rest * 43) >> 8
    place = (row >> 5) & 7
    step = jnp.zeros_like(row)
    for n, d in enumerate(FAR_FIRST):
        step = jnp.where(place == n, d, step)
    zrow = (z + step) & 7
    yrow = jnp.where(row < 256, 1 - y, y)
    col = 192 * x + 96 * yrow + 12 * zrow + 6 * core + rest - 6 * tap
    col = jnp.where(tap < TAPS, col, -1)
    lane = lax.broadcasted_iota(I32, (512, FULL), 1)
    chosen = jnp.where(lane == col, 1.0, 0.0).astype(BF16)
    table = dot(chosen, w40b[...], ((1,), (1,)))
    placed = jnp.zeros((512, 128), F32)
    for k in range(TAPS):
        moved = table if k == 0 else pltpu.roll(table, 8 * k, 1)
        placed = jnp.where(tap == k, moved, placed)
    sel_ref[...] = placed.astype(BF16)

    load_cot.wait()
    for k in range(TAPS):
        loads[k].wait()
        grow[:, FULL * k : FULL * (k + 1)] = dot(gall[0], w_ref[k], ((1,), (1,)))

    load_tok.wait()
    tok_sib.wait_recv()
    tok_out.wait_recv()
    near = jnp.broadcast_to(toks[0], (8, ROWS))
    far = jnp.broadcast_to(toks[1], (8, ROWS))
    own = jnp.broadcast_to(tok_ref[...], (8, ROWS))
    left = jnp.where(core == 1, near, far)
    right = jnp.where(core == 1, far, near)
    left = jnp.where(seq == 0, OUTSIDE, left)
    right = jnp.where(seq == 127, OUTSIDE, right)
    row3 = jnp.concatenate([left, own, right], axis=1)
    wins[0] = pltpu.roll(row3, 3 * ROWS - 124, 1)[:, :256]
    letter = lax.broadcasted_iota(I32, (8, ROWS), 0)

    def one_hots(b):
        win = wins[b]
        for i in range(9):
            ids = win[:, :ROWS] if i == 0 else pltpu.roll(win, 256 - i, 1)[:, :ROWS]
            ohf[8 * i : 8 * i + 8, :ROWS] = jnp.where(ids == letter, 1.0, 0.0)
            turned = jnp.where(ids == OUTSIDE, OUTSIDE, 3 - ids)
            ohf[64 - 8 * i : 72 - 8 * i, ROWS:] = jnp.where(turned == letter, 1.0, 0.0)
        ohb[:, 256 * b : 256 * b + 256] = ohf[...].astype(BF16)

    one_hots(0)
    for k in range(TAPS):
        hots[:, 256 * k : 256 * k + 256] = ohf[8 * k : 8 * k + 40, :].astype(BF16)

    def own_tap(k):
        hot = hots[:, 256 * k : 256 * k + 256]
        stm[...] = dot(hot, w40b[0:40, :], ((0,), (0,))).astype(BF16)
        if k == 2:
            half = pl.ds(pl.multiple_of(chan * HALF, 128), HALF)
            rown[0:ROWS, :] = f32(stm[0:ROWS, half]) + f32(stm[ROWS:, half])

        def strip(n, _):
            top = pl.ds(pl.multiple_of(n * 32, 32), 32)
            for c in range(0, FULL, 256):
                cols = slice(c, c + 256)
                wide = slice(FULL * k + c, FULL * k + c + 256)
                grad = grow[top, wide]
                total = None
                for side in range(2):
                    v = f32(stm[pl.ds(pl.multiple_of(n * 32 + ROWS * side, 32), 32), cols])
                    v2 = v * v
                    h = gelu_half(v, v2)
                    act = v * h
                    total = act if total is None else total + act
                    slope = h + (act - act * h) * (2.0 * C0 + 6.0 * C1 * v2)
                    into = pl.ds(pl.multiple_of(n * 32 + 256 * k + ROWS * side, 32), 32)
                    dsb[into, cols] = (grad * slope).astype(BF16)
                skb[top, wide] = total.astype(BF16)
            return 0

        lax.fori_loop(0, ROWS // 32, strip, 0, unroll=True)

    own_tap(0)
    s_win = [
        send(wins.at[0], wins.at[4 * dc + d], across(d, 0, dc))
        for d, dc in ((2, 0), (2, 1), (1, 0), (3, 0), (1, 1), (3, 1), (0, 1))
    ]
    own_tap(1)
    halves = []
    for d, half in ((1, 0), (3, 1)):
        g_x[d].wait_recv()
        rows = pl.ds(64 * half, 64)
        for dc in range(2):
            into = gall.at[2 + 4 * dc, rows]
            halves.append(send(gall.at[d, rows], into, across(d, 0, dc)))
        g_sib[d] = send(gall.at[d], gall.at[4 + d], sibling)
    for k in range(2, TAPS):
        own_tap(k)

    gsacc = dot(hots[...], dsb[...], ((1,), (0,)))
    for h in range(2):
        for j in range(TAPS):
            for t in range(3):
                c = HALF * h + 128 * t
                gsend[h, 3 * j + t] = gsacc[8 * j : 8 * j + 8, c : c + 128]
        gsend[h, 15] = jnp.zeros((8, 128), F32)
    mine = 2 * x + core
    me = 8 * chan + 4 * core + x
    grz[me] = gsend[chan, pl.ds(2 * mine, 2)]
    s_z = []
    for dx, dy, dc, dh in halves_of:
        owner = 2 * lax.rem(x + dx, NX) + (1 - core if dc else core)
        part = gsend.at[1 - chan if dh else chan, pl.ds(2 * owner, 2)]
        s_z.append(send(part, grz.at[me], across(dx, dy, dc, dh)))

    def blocks(first, side):
        here = slice(256 * first, 256 * first + 1024)
        part = slice(256 * side, 256 * side + 256)
        stt[part, :] = dot(sel_ref[part, :], ohb[:, here], ((1,), (0,))).astype(BF16)

        def strip(n, _):
            rows = pl.ds(pl.multiple_of(256 * side + n * 64, 64), 64)
            for b in range(4):
                v = f32(stt[rows, 256 * b : 256 * b + 256])
                act = v * gelu_half(v, v * v)
                into = slice((first + b) * ROWS, (first + b + 1) * ROWS)
                st[rows, into] = (act[:, :ROWS] + act[:, ROWS:]).astype(BF16)
            return 0

        lax.fori_loop(0, 256 // 64, strip, 0, unroll=True)

    for copy in s_win:
        copy.wait_recv()
    for b in range(1, 8):
        one_hots(b)
    blocks(0, 0)
    blocks(4, 0)
    for copy in halves + list(g_sib.values()):
        copy.wait_recv()
    every = gall[...].reshape(8 * ROWS, HALF)
    s_y = []
    for n, (first, last) in enumerate(CHUNKS):
        rows = slice(32 * first, 32 * last)
        span = pl.ds(32 * first, 32 * (last - first))
        rsend[rows, :] = dot(st[rows, :], every, ((1,), (0,))).astype(BF16)
        s_y.append(send(rsend.at[span], ry.at[span], beside_y))
    blocks(0, 1)
    blocks(4, 1)
    for copy in s_z:
        copy.wait_recv()
    part = grz[0]
    for n in range(1, 16):
        part = part + grz[n]
    gone[...] = part
    grx[z] = part
    s_gx = [send(gone, grx.at[z], z_by(d)) for d in FAR_FIRST[:-1]]

    conv = rown[0:ROWS, :]
    conv += dot(skb[...], w_ref[...].reshape(TAPS * FULL, HALF), ((1,), (0,)))
    bl_ref[...] = (0.5 * conv).astype(BF16)
    rown[...] = dot(st[256:, :], every, ((1,), (0,)))

    s_rz = []
    for n, (first, last) in enumerate(CHUNKS):
        if n == 3:
            for copy in s_gx:
                copy.wait_recv()
            parts = [grx[m] for m in range(NZ)]
            while len(parts) > 1:
                parts = [p + q for p, q in zip(parts[0::2], parts[1::2])]
            whole = gfin.at[y, pl.ds(2 * mine, 2)]
            whole[...] = 0.5 * parts[0]
            s_gf = [send(whole, whole, across(*s)) for s in sides_of]
        s_y[n].wait_recv()
        rows = slice(32 * first, 32 * last)
        both = rown[rows, :] + ry[rows, :].astype(F32)
        if n == 3:
            rown[rows, :] = both
        zsend[rows, :] = both.astype(BF16)
        for m in range(first, last):
            d = FAR_FIRST[m]
            if d:
                s_rz.append(send(zsend.at[pl.ds(32 * m, 32)], zrecv.at[d], z_by(d)))


    for copy in s_rz:
        copy.wait_recv()
    total = rown[224:256, :]
    for d in range(1, NZ):
        total = total + zrecv[d].astype(F32)
    total = 0.5 * total
    for k in range(TAPS):
        gc_ref[k] = total[6 * k : 6 * k + 6, :]
    for copy in s_gf:
        copy.wait_recv()
    for j in range(TAPS):
        for t in range(3):
            gs_ref[j, :, 128 * t : 128 * t + 128] = gfin[0, 3 * j + t, 0:4, :] + gfin[1, 3 * j + t, 0:4, :]
    for copy in used:
        copy.wait_send()


def on_device(tokens, stem_weight, conv_weight, cotangent):
    vmem = pl.BlockSpec(memory_space=pltpu.VMEM)
    hbm = pl.BlockSpec(memory_space=pltpu.HBM)
    V = pltpu.VMEM
    return pl.pallas_call(
        kernel,
        out_shape=(
            jax.ShapeDtypeStruct((ROWS, HALF), BF16),
            jax.ShapeDtypeStruct((TAPS, 6, HALF), F32),
            jax.ShapeDtypeStruct((TAPS, 4, HALF), F32),
        ),
        in_specs=[hbm, hbm, hbm, hbm],
        out_specs=(vmem, vmem, vmem),
        scratch_shapes=[
            V((TAPS, FULL, HALF), BF16), V((1, ROWS), I32), V((TAPS, 4, FULL), BF16),
            V((2, 1, ROWS), I32), V((8, 8, 256), I32),
            V((8, ROWS, HALF), BF16), V((128, FULL), F32), V((128, FULL), BF16),
            V((512, 128), BF16), V((128, 256), F32), V((128, 2048), BF16), V((40, 1280), BF16),
            V((256, FULL), BF16), V((ROWS, TAPS * FULL), F32),
            V((ROWS, TAPS * FULL), BF16), V((TAPS * 256, FULL), BF16),
            V((512, 1024), BF16), V((512, 1024), BF16), V((256, HALF), BF16),
            V((256, HALF), F32), V((256, HALF), BF16), V((256, HALF), BF16), V((8, 32, HALF), BF16),
            V((2, 16, 8, 128), F32), V((16, 2, 8, 128), F32),
            V((2, 8, 128), F32), V((NZ, 2, 8, 128), F32), V((NY, 16, 8, 128), F32),
            pltpu.SemaphoreType.DMA((8,)), pltpu.SemaphoreType.DMA((96,)),
            pltpu.SemaphoreType.DMA((96,)),
        ],
        compiler_params=pltpu.CompilerParams(
            collective_id=0, has_side_effects=True, vmem_limit_bytes=48 * 2**20
        ),
    )(tokens.reshape(1, ROWS), stem_weight, conv_weight, cotangent)


def solution(mesh):
    return jax.shard_map(
        on_device,
        mesh=mesh,
        in_specs=(P("seq"), P(), P(None, None, "chan"), P("seq", "chan")),
        out_specs=(P("seq", "chan"), P(None, "seq", "chan"), P(None, None, "chan")),
        check_vma=False,
    )
```

```python
import math

import jax
import jax.numpy as jnp
from jax import lax
from jax.experimental import pallas as pl
from jax.experimental.pallas import tpu as pltpu
from jax.sharding import PartitionSpec as P

F32, BF16, I32 = jnp.float32, jnp.bfloat16, jnp.int32
C0 = math.sqrt(2.0 / math.pi)
C1 = C0 * 0.044715
OUTSIDE = 4
FAR_FIRST = (4, 3, 5, 2, 6, 1, 7, 0)
CHUNKS = ((0, 4), (4, 7), (7, 8))
ROWS, FULL, HALF, TAPS = 128, 768, 384, 5
NX, NY, NZ = 4, 2, 8


def dot(a, b, dims):
    return lax.dot_general(a, b, (dims, ((), ())), preferred_element_type=F32)


def f32(v):
    return v.astype(F32)


def gelu_half(v, v2):
    return 0.5 + 0.5 * jnp.tanh(v * (C0 + C1 * v2))


def kernel(
    tok_hbm, sw_hbm, w_hbm, cot_hbm,
    bl_ref, gc_ref, gs_ref,
    w_ref, tok_ref, sw_ref, toks, wins, gall, w40, w40b, sel_ref, ohf, ohb, hots, stm, grow, skb, dsb,
    stt, st, rsend, rown, ry, zsend, zrecv,
    gsend, grz, gone, grx, gfin,
    wsem, ssem, rsem,
):
    seq, chan = lax.axis_index("seq"), lax.axis_index("chan")
    core = lax.rem(seq, 2)
    z = lax.rem(lax.div(seq, 2), NZ)
    y = lax.rem(lax.div(seq, 2 * NZ), NY)
    x = lax.div(seq, 2 * NZ * NY)

    def at(px, py, pz, pc, ch):
        return (((px * NY + py) * NZ + pz) * 2 + pc, ch)

    def x_by(d):
        return at(lax.rem(x + d, NX), y, z, core, chan)

    def z_by(d):
        return at(x, y, lax.rem(z + d, NZ), core, chan)

    def across(dx, dy, dc, dh=0):
        return at(
            lax.rem(x + dx, NX), 1 - y if dy else y, z, 1 - core if dc else core,
            1 - chan if dh else chan,
        )

    sibling = across(0, 0, 1)
    beside_y = across(0, 1, 0)
    outer = (lax.rem(seq + 128 + 2 * core - 1, 128), chan)
    cores = [(dx, dc) for dx in (2, 1, 3, 0) for dc in (1, 0)]
    halves_of = [(dx, 0, dc, dh) for dh in (1, 0) for dx, dc in cores][:-1]
    sides_of = [(dx, dy, dc) for dy in (1, 0) for dx, dc in cores][:-1]
    partners = [outer] + [across(*s) for s in halves_of] + [across(*s) for s in sides_of[:8]]
    partners += [z_by(d) for d in FAR_FIRST[:-1]]

    barrier = pltpu.get_barrier_semaphore()
    for device in partners:
        pl.semaphore_signal(
            barrier, inc=1, device_id=device, device_id_type=pl.DeviceIdType.MESH
        )

    used = []

    def send(src, dst, device):
        n = len(used)
        copy = pltpu.make_async_remote_copy(
            src_ref=src, dst_ref=dst, send_sem=ssem.at[n], recv_sem=rsem.at[n],
            device_id=device, device_id_type=pl.DeviceIdType.MESH,
        )
        copy.start()
        used.append(copy)
        return copy

    def load(n, src, dst):
        copy = pltpu.make_async_copy(src, dst, wsem.at[n])
        copy.start()
        return copy

    load_tok = load(5, tok_hbm, tok_ref)
    load_sw = load(6, sw_hbm, sw_ref)
    load_cot = load(7, cot_hbm, gall.at[0])
    loads = [load(k, w_hbm.at[k], w_ref.at[k]) for k in range(TAPS)]

    w40[...] = jnp.zeros_like(w40)
    ohf[...] = jnp.zeros_like(ohf)
    pl.semaphore_wait(barrier, len(partners))

    tok_out = send(tok_hbm, toks.at[1], outer)
    tok_sib = send(tok_hbm, toks.at[0], sibling)
    g_x = {d: send(cot_hbm, gall.at[d], x_by(d)) for d in (1, 3)}
    g_sib = {0: send(cot_hbm, gall.at[4], sibling)}

    load_sw.wait()
    for j in range(TAPS):
        w40[8 * j : 8 * j + 4, :] = sw_ref[j].astype(F32)
    w40[20:21, :] = jnp.full((1, FULL), -128.0, F32)
    w40b[...] = w40[...].astype(BF16)

    row = lax.broadcasted_iota(I32, (512, 1), 0)
    rest = row & 31
    tap = (rest * 43) >> 8
    place = (row >> 5) & 7
    step = jnp.zeros_like(row)
    for n, d in enumerate(FAR_FIRST):
        step = jnp.where(place == n, d, step)
    zrow = (z + step) & 7
    yrow = jnp.where(row < 256, 1 - y, y)
    col = 192 * x + 96 * yrow + 12 * zrow + 6 * core + rest - 6 * tap
    col = jnp.where(tap < TAPS, col, -1)
    lane = lax.broadcasted_iota(I32, (512, FULL), 1)
    chosen = jnp.where(lane == col, 1.0, 0.0).astype(BF16)
    table = dot(chosen, w40b[...], ((1,), (1,)))
    placed = jnp.zeros((512, 128), F32)
    for k in range(TAPS):
        moved = table if k == 0 else pltpu.roll(table, 8 * k, 1)
        placed = jnp.where(tap == k, moved, placed)
    sel_ref[...] = placed.astype(BF16)

    load_cot.wait()
    for k in range(TAPS):
        loads[k].wait()
        grow[:, FULL * k : FULL * (k + 1)] = dot(gall[0], w_ref[k], ((1,), (1,)))

    load_tok.wait()
    tok_sib.wait_recv()
    tok_out.wait_recv()
    near = jnp.broadcast_to(toks[0], (8, ROWS))
    far = jnp.broadcast_to(toks[1], (8, ROWS))
    own = jnp.broadcast_to(tok_ref[...], (8, ROWS))
    left = jnp.where(core == 1, near, far)
    right = jnp.where(core == 1, far, near)
    left = jnp.where(seq == 0, OUTSIDE, left)
    right = jnp.where(seq == 127, OUTSIDE, right)
    row3 = jnp.concatenate([left, own, right], axis=1)
    wins[0] = pltpu.roll(row3, 3 * ROWS - 124, 1)[:, :256]
    letter = lax.broadcasted_iota(I32, (8, ROWS), 0)

    def one_hots(b):
        win = wins[b]
        for i in range(9):
            ids = win[:, :ROWS] if i == 0 else pltpu.roll(win, 256 - i, 1)[:, :ROWS]
            ohf[8 * i : 8 * i + 8, :ROWS] = jnp.where(ids == letter, 1.0, 0.0)
            turned = jnp.where(ids == OUTSIDE, OUTSIDE, 3 - ids)
            ohf[64 - 8 * i : 72 - 8 * i, ROWS:] = jnp.where(turned == letter, 1.0, 0.0)
        ohb[:, 256 * b : 256 * b + 256] = ohf[...].astype(BF16)

    one_hots(0)
    for k in range(TAPS):
        hots[:, 256 * k : 256 * k + 256] = ohf[8 * k : 8 * k + 40, :].astype(BF16)

    def own_tap(k):
        hot = hots[:, 256 * k : 256 * k + 256]
        stm[...] = dot(hot, w40b[0:40, :], ((0,), (0,))).astype(BF16)
        if k == 2:
            half = pl.ds(pl.multiple_of(chan * HALF, 128), HALF)
            rown[0:ROWS, :] = f32(stm[0:ROWS, half]) + f32(stm[ROWS:, half])

        def strip(n, _):
            top = pl.ds(pl.multiple_of(n * 32, 32), 32)
            for c in range(0, FULL, 256):
                cols = slice(c, c + 256)
                wide = slice(FULL * k + c, FULL * k + c + 256)
                grad = grow[top, wide]
                total = None
                for side in range(2):
                    v = f32(stm[pl.ds(pl.multiple_of(n * 32 + ROWS * side, 32), 32), cols])
                    v2 = v * v
                    h = gelu_half(v, v2)
                    act = v * h
                    total = act if total is None else total + act
                    slope = h + (act - act * h) * (2.0 * C0 + 6.0 * C1 * v2)
                    into = pl.ds(pl.multiple_of(n * 32 + 256 * k + ROWS * side, 32), 32)
                    dsb[into, cols] = (grad * slope).astype(BF16)
                skb[top, wide] = total.astype(BF16)
            return 0

        lax.fori_loop(0, ROWS // 32, strip, 0, unroll=True)

    own_tap(0)
    s_win = [
        send(wins.at[0], wins.at[4 * dc + d], across(d, 0, dc))
        for d, dc in ((2, 0), (2, 1), (1, 0), (3, 0), (1, 1), (3, 1), (0, 1))
    ]
    own_tap(1)
    halves = []
    for d, half in ((1, 0), (3, 1)):
        g_x[d].wait_recv()
        rows = pl.ds(64 * half, 64)
        for dc in range(2):
            into = gall.at[2 + 4 * dc, rows]
            halves.append(send(gall.at[d, rows], into, across(d, 0, dc)))
        g_sib[d] = send(gall.at[d], gall.at[4 + d], sibling)
    for k in range(2, TAPS):
        own_tap(k)

    gsacc = dot(hots[...], dsb[...], ((1,), (0,)))
    for h in range(2):
        for j in range(TAPS):
            for t in range(3):
                c = HALF * h + 128 * t
                gsend[h, 3 * j + t] = gsacc[8 * j : 8 * j + 8, c : c + 128]
        gsend[h, 15] = jnp.zeros((8, 128), F32)
    mine = 2 * x + core
    me = 8 * chan + 4 * core + x
    grz[me] = gsend[chan, pl.ds(2 * mine, 2)]
    s_z = []
    for dx, dy, dc, dh in halves_of:
        owner = 2 * lax.rem(x + dx, NX) + (1 - core if dc else core)
        part = gsend.at[1 - chan if dh else chan, pl.ds(2 * owner, 2)]
        s_z.append(send(part, grz.at[me], across(dx, dy, dc, dh)))

    def blocks(first, side):
        here = slice(256 * first, 256 * first + 1024)
        part = slice(256 * side, 256 * side + 256)
        stt[part, :] = dot(sel_ref[part, :], ohb[:, here], ((1,), (0,))).astype(BF16)

        def strip(n, _):
            rows = pl.ds(pl.multiple_of(256 * side + n * 64, 64), 64)
            for b in range(4):
                v = f32(stt[rows, 256 * b : 256 * b + 256])
                act = v * gelu_half(v, v * v)
                into = slice((first + b) * ROWS, (first + b + 1) * ROWS)
                st[rows, into] = (act[:, :ROWS] + act[:, ROWS:]).astype(BF16)
            return 0

        lax.fori_loop(0, 256 // 64, strip, 0, unroll=True)

    for copy in s_win:
        copy.wait_recv()
    for b in range(1, 8):
        one_hots(b)
    blocks(0, 0)
    blocks(4, 0)
    for copy in halves + list(g_sib.values()):
        copy.wait_recv()
    every = gall[...].reshape(8 * ROWS, HALF)
    s_y = []
    for n, (first, last) in enumerate(CHUNKS):
        rows = slice(32 * first, 32 * last)
        span = pl.ds(32 * first, 32 * (last - first))
        rsend[rows, :] = dot(st[rows, :], every, ((1,), (0,))).astype(BF16)
        s_y.append(send(rsend.at[span], ry.at[span], beside_y))
    blocks(0, 1)
    blocks(4, 1)
    for copy in s_z:
        copy.wait_recv()
    part = grz[0]
    for n in range(1, 16):
        part = part + grz[n]
    gone[...] = part
    grx[z] = part
    s_gx = [send(gone, grx.at[z], z_by(d)) for d in FAR_FIRST[:-1]]

    conv = rown[0:ROWS, :]
    conv += dot(skb[...], w_ref[...].reshape(TAPS * FULL, HALF), ((1,), (0,)))
    bl_ref[...] = (0.5 * conv).astype(BF16)
    rown[...] = dot(st[256:, :], every, ((1,), (0,)))

    s_rz = []
    for n, (first, last) in enumerate(CHUNKS):
        if n == len(CHUNKS) - 1:
            for copy in s_gx:
                copy.wait_recv()
            parts = [grx[m] for m in range(NZ)]
            while len(parts) > 1:
                parts = [p + q for p, q in zip(parts[0::2], parts[1::2])]
            whole = gfin.at[y, pl.ds(2 * mine, 2)]
            whole[...] = 0.5 * parts[0]
            s_gf = [send(whole, whole, across(*s)) for s in sides_of]
        s_y[n].wait_recv()
        rows = slice(32 * first, 32 * last)
        both = rown[rows, :] + ry[rows, :].astype(F32)
        if n == len(CHUNKS) - 1:
            rown[rows, :] = both
        zsend[rows, :] = both.astype(BF16)
        for m in range(first, last):
            d = FAR_FIRST[m]
            if d:
                s_rz.append(send(zsend.at[pl.ds(32 * m, 32)], zrecv.at[d], z_by(d)))


    for copy in s_rz:
        copy.wait_recv()
    total = rown[224:256, :]
    for d in range(1, NZ):
        total = total + zrecv[d].astype(F32)
    total = 0.5 * total
    for k in range(TAPS):
        gc_ref[k] = total[6 * k : 6 * k + 6, :]
    for copy in s_gf:
        copy.wait_recv()
    for j in range(TAPS):
        for t in range(3):
            gs_ref[j, :, 128 * t : 128 * t + 128] = gfin[0, 3 * j + t, 0:4, :] + gfin[1, 3 * j + t, 0:4, :]
    for copy in used:
        copy.wait_send()


def on_device(tokens, stem_weight, conv_weight, cotangent):
    vmem = pl.BlockSpec(memory_space=pltpu.VMEM)
    hbm = pl.BlockSpec(memory_space=pltpu.HBM)
    V = pltpu.VMEM
    return pl.pallas_call(
        kernel,
        out_shape=(
            jax.ShapeDtypeStruct((ROWS, HALF), BF16),
            jax.ShapeDtypeStruct((TAPS, 6, HALF), F32),
            jax.ShapeDtypeStruct((TAPS, 4, HALF), F32),
        ),
        in_specs=[hbm, hbm, hbm, hbm],
        out_specs=(vmem, vmem, vmem),
        scratch_shapes=[
            V((TAPS, FULL, HALF), BF16), V((1, ROWS), I32), V((TAPS, 4, FULL), BF16),
            V((2, 1, ROWS), I32), V((8, 8, 256), I32),
            V((8, ROWS, HALF), BF16), V((128, FULL), F32), V((128, FULL), BF16),
            V((512, 128), BF16), V((128, 256), F32), V((128, 2048), BF16), V((40, 1280), BF16),
            V((256, FULL), BF16), V((ROWS, TAPS * FULL), F32),
            V((ROWS, TAPS * FULL), BF16), V((TAPS * 256, FULL), BF16),
            V((512, 1024), BF16), V((512, 1024), BF16), V((256, HALF), BF16),
            V((256, HALF), F32), V((256, HALF), BF16), V((256, HALF), BF16), V((8, 32, HALF), BF16),
            V((2, 16, 8, 128), F32), V((16, 2, 8, 128), F32),
            V((2, 8, 128), F32), V((NZ, 2, 8, 128), F32), V((NY, 16, 8, 128), F32),
            pltpu.SemaphoreType.DMA((8,)), pltpu.SemaphoreType.DMA((96,)),
            pltpu.SemaphoreType.DMA((96,)),
        ],
        compiler_params=pltpu.CompilerParams(
            collective_id=0, has_side_effects=True, vmem_limit_bytes=48 * 2**20
        ),
    )(tokens.reshape(1, ROWS), stem_weight, conv_weight, cotangent)


def solution(mesh):
    return jax.shard_map(
        on_device,
        mesh=mesh,
        in_specs=(P("seq"), P(), P(None, None, "chan"), P("seq", "chan")),
        out_specs=(P("seq", "chan"), P(None, "seq", "chan"), P(None, None, "chan")),
        check_vma=False,
    )
```
